512 devices in a mesh: brick: 64 (over z, y), freq: 8 (over x, core).
Axes of the slice: x: 4, y: 8, z: 8, core: 2. Of those that a mesh axis runs over, the one named last changes fastest.
Arguments:
- forward_fields: bfloat16 [8, 64, 2, 512, 1536], P('freq', 'brick'), may hold values from -6 to 6
- adjoint_panels: bfloat16 [8, 16384, 2, 1536], P('freq', 'brick'), may hold values from -6 to 6
- residual_blocks: bfloat16 [8, 64, 8, 3, 64, 128], P('freq', 'brick'), may hold values from -0.0048828125 to 0.0048828125
- residual_columns: int32 [64, 8, 3], P('brick'), may hold values from 0 to 7, as said below
- panel_brick: int32 [16384, 1], P('brick'), may hold values from 0 to 63; in each aligned block of 256 rows (0 to 255, 256 to 511, ...) at most 8 rows name the same one
- panel_receiver: int32 [16384], P('brick'), may hold values from 0 to 511
Outputs:
- gradient: float32 [32768], P(('brick', 'freq'))
The draws below stay inside these ranges and needn't reach their ends.
Inputs may be any that keep to these rules, and one draw needn't show every extreme that they name: `panel_brick`: the panels of one device lie on any one brick at most 8 times, and on some brick exactly 8 times. `residual_columns`: the 3 receiver blocks of one transmitter block follow one another cyclically modulo 8.
All inputs are finite; a program needn't handle non-finite values.
Results may differ from the reference program's by a relative error of at most 0.0003.
Values may be sent and summed in bfloat16 or wider, within the bound.
A program may use at most 64 MiB of HBM per device.

```python
import math
import jax
import jax.numpy as jnp
import numpy as np
from jax import lax

CELLS = 512
TXB_DEV = 8
P_DEV = 256
BLK = 64
NBLK = 3
RXB = 8
RX = 512
TXL = 512
CAP = 8
BRICKS = 64
NF = 8
PANELS = 16384


def draw_residual_columns(key, part):
    start = jax.random.randint(key, (BRICKS, TXB_DEV, 1), 0, RXB)
    return ((start + jnp.arange(NBLK, dtype=jnp.int32)[None, None, :]) % RXB).astype(jnp.int32)


def plant(values, own_key, smallest, top_value):
    longest = values.shape.index(max(values.shape))
    spots = []
    for shift in (0, 1):
        where = [jax.random.randint(jax.random.fold_in(own_key, axis), (), 0, length) for axis, length in enumerate(values.shape)]
        where[longest] = (where[longest] + shift) % values.shape[longest]
        spots.append(tuple(where))
    return values.at[spots[0]].set(smallest).at[spots[1]].set(top_value)


def block_levels(own_key, extent, shards, smallest, high):
    loudness = 1.0
    for position, shards_of in shards:
        draws = jax.random.uniform(jax.random.fold_in(jax.random.fold_in(own_key, 6), position), (shards_of,), jnp.float32, smallest / len(shards), high / len(shards))
        loudness = loudness * jnp.repeat(jnp.exp(draws), extent[position] // shards_of).reshape((-1,) + (1,) * (len(extent) - 1 - position))
    return loudness


def shared_out(own_key, own, number, rows, count, top, most, lean):
    sequence = jax.random.permutation(own_key, count)
    packed, usual = load_shares(count, rows * top, most, lean, True), load_shares(count, rows * top, most, lean, False)
    places = jnp.arange(count)

    def named(sizes, rotation):
        used = int((sizes > 0).sum())
        fixed = max(1, used // 4)
        moved = fixed + (places - fixed + rotation * (used - fixed)) % max(1, count - fixed)
        return jnp.zeros((count,), jnp.int32).at[sequence[jnp.where(places < fixed, places, moved)]].set(jnp.asarray(sizes, jnp.int32))

    sizes = jnp.where(number % 4 == 0, named(packed, number // 4), named(usual, number - number // 4 - 1))
    mixed = jax.random.permutation(jax.random.fold_in(own, 3), count)
    donor, receiver = mixed[0:count // 2 * 2:2], mixed[1:count // 2 * 2:2]
    room = jnp.minimum(sizes[donor] - 1, most - sizes[receiver]) // 2
    room = jnp.where((donor == sequence[0]) | (receiver == sequence[0]) | (sizes[receiver] == 0), 0, jnp.maximum(room, 0))
    moved = jax.random.randint(jax.random.fold_in(own, 4), (count // 2,), 0, 1 << 20) % (room + 1)
    sizes = sizes.at[donor].add(-moved).at[receiver].add(moved)
    labels = jnp.searchsorted(jnp.cumsum(sizes), jnp.arange(rows * top), side="right").astype(jnp.int32)
    grid = labels.reshape(top, rows).T
    grid = grid[jax.random.permutation(jax.random.fold_in(own, 1), rows)]
    rotation = jax.random.randint(jax.random.fold_in(own, 2), (rows, 1), 0, top)
    return jnp.take_along_axis(grid, (jnp.arange(top)[None, :] + rotation) % top, axis=1)


def load_shares(count, total, bound, skew, full):
    loads = [(1 << 20) // math.isqrt(standing ** skew) + 1 for standing in range(1, count + 1)]
    largest = bound if full else min(bound, max(-(-total // count), total * loads[0] // sum(loads)))
    least = 1 if total - largest >= count - 1 else 0
    given, spare = [largest] + [least] * (count - 1), total - largest - least * (count - 1)
    while spare > 0:
        movable = [i for i in range(1, count) if given[i] < largest] or [i for i in range(1, count) if given[i] < bound]
        mass, left = sum([loads[i] for i in movable]), spare
        for i in movable:
            addition = min(bound - given[i], max(1, left * loads[i] // mass), spare)
            given[i] = given[i] + addition
            spare = spare - addition
    return np.array(given)


def scatter_about(stream_key, extent, scale, limit, pieces=(), kind=jnp.bfloat16):
    values = scale * jax.random.normal(stream_key, extent, jnp.float32)
    if pieces:
        values = values * block_levels(stream_key, extent, pieces, -0.22, 0.18)
    return jnp.clip(values, -limit, limit).astype(kind)


def setup_inputs(seed: int = 0) -> dict:
    key_of = jax.random.split(jax.random.key(seed), 7)
    forward_fields = scatter_about(key_of[0], (NF, BRICKS, 2, TXL, 3 * CELLS), 1.0, 6.0, ((0, 8), (1, 64)))
    adjoint_panels = scatter_about(key_of[1], (NF, PANELS, 2, 3 * CELLS), 1.0, 6.0, ((0, 8), (1, 64)))
    residual_blocks = scatter_about(key_of[2], (NF, BRICKS, TXB_DEV, NBLK, BLK, 2 * BLK), (1.0 / (8.0 * (TXL * P_DEV) ** 0.5)), 0.0048828125, ((0, 8), (1, 64)))
    residual_columns = draw_residual_columns(jax.random.fold_in(key_of[6], 71), 0)
    panel_brick_keys = jax.random.split(jax.random.fold_in(key_of[4], 1), PANELS // P_DEV)
    panel_brick_turns = jax.random.permutation(jax.random.fold_in(key_of[4], 3), PANELS // P_DEV)
    panel_brick = jax.vmap(lambda own, number: shared_out(jax.random.fold_in(key_of[4], 2), own, number, P_DEV, BRICKS, 1, CAP, 2))(panel_brick_keys, panel_brick_turns).reshape((PANELS, 1))
    panel_receiver = plant(jax.random.randint(key_of[5], (PANELS,), 0, RX), jax.random.fold_in(key_of[5], 1), 0, RX - 1).astype(jnp.int32)
    return dict(forward_fields=forward_fields, adjoint_panels=adjoint_panels, residual_blocks=residual_blocks, residual_columns=residual_columns, panel_brick=panel_brick, panel_receiver=panel_receiver)


def pick_columns(blocks, columns, receivers):
    width = blocks.shape[-2]
    rblock = jnp.where(receivers >= 0, receivers // width, -1).astype(jnp.int32)
    offset = (receivers % width).astype(jnp.int32)
    match = (columns[:, :, None] == rblock[None, None, :]).astype(jnp.float32)
    onehot = (jnp.arange(width, dtype=jnp.int32)[:, None] == offset[None, :]).astype(jnp.float32)
    values = blocks.astype(jnp.float32)
    real_part = jnp.einsum("kjto,os->kjts", values[..., :width], onehot, precision=lax.Precision.HIGHEST)
    imag_part = jnp.einsum("kjto,os->kjts", values[..., width:], onehot, precision=lax.Precision.HIGHEST)
    real_col = jnp.einsum("kjts,kjs->kts", real_part, match, precision=lax.Precision.HIGHEST)
    imag_col = jnp.einsum("kjts,kjs->kts", imag_part, match, precision=lax.Precision.HIGHEST)
    count = real_col.shape[0] * real_col.shape[1]
    real_col = real_col.reshape(count, -1).astype(jnp.bfloat16)
    imag_col = imag_col.reshape(count, -1).astype(jnp.bfloat16)
    return real_col, imag_col


def correlate(real_col, imag_col, fields, panels):
    slots = real_col.shape[1]
    left = jnp.concatenate([jnp.concatenate([real_col.T, -imag_col.T], axis=1), jnp.concatenate([imag_col.T, real_col.T], axis=1)], axis=0)
    right = fields.reshape(-1, fields.shape[-1])
    product = jnp.dot(left, right, preferred_element_type=jnp.float32)
    per_panel = product[:slots] * panels[:, 0].astype(jnp.float32) - product[slots:] * panels[:, 1].astype(jnp.float32)
    return per_panel.reshape(slots, 3, -1).sum(axis=1)


def reference(forward_fields, adjoint_panels, residual_blocks, residual_columns, panel_brick, panel_receiver):
    slots = BRICKS * CAP
    target = panel_brick[:, 0]

    def one_brick(brick_id):
        found = jnp.nonzero(target == brick_id, size=slots, fill_value=PANELS)[0].astype(jnp.int32)
        valid = found < PANELS
        safe = jnp.minimum(found, PANELS - 1).astype(jnp.int32)
        receivers = jnp.where(valid, panel_receiver[safe], -1).astype(jnp.int32)
        columns = residual_columns[brick_id]
        total = jnp.zeros((CELLS,), jnp.float32)
        for freq_id in range(NF):
            panels = jnp.where(valid[:, None, None], adjoint_panels[freq_id][safe], jnp.zeros((), jnp.bfloat16))
            real_col, imag_col = pick_columns(residual_blocks[freq_id, brick_id], columns, receivers)
            total = total + correlate(real_col, imag_col, forward_fields[freq_id, brick_id], panels).sum(axis=0)
        return total

    result = lax.map(one_brick, jnp.arange(BRICKS, dtype=jnp.int32))
    return result.reshape(-1)
```

```python
import functools

import jax
import jax.numpy as jnp
from jax import lax
from jax.experimental import pallas as pl
from jax.experimental.pallas import tpu as pltpu
from jax.sharding import PartitionSpec as P

SIDE = 8
SLOTS = 8
MESH = pl.DeviceIdType.MESH


def zigzag(step):
    half = (step + 1) // 2
    return 4 + half * (1 - 2 * lax.rem(step, 2))


def kernel(
    bricks, freqs, columns_ref, target_ref, receiver_ref, panels_hbm, fields_hbm, blocks_hbm,
    out_ref,
    panels, fields, blocks, outgoing, incoming, labels_out, labels_in, dense, left, product,
    total, partial, gathered,
    load_sem, send_sem, recv_sem, label_send_sem, label_recv_sem, sum_send_sem, sum_recv_sem,
):
    me = lax.axis_index("brick")
    mine = lax.axis_index("freq")
    my_z, my_y = me // SIDE, lax.rem(me, SIDE)
    held, width = panels.shape
    span = fields.shape[1]
    cells = span // 3
    tx = fields.shape[0] // 2

    loads = [
        pltpu.make_async_copy(panels_hbm, panels, load_sem.at[0]),
        pltpu.make_async_copy(blocks_hbm, blocks, load_sem.at[1]),
        pltpu.make_async_copy(fields_hbm, fields, load_sem.at[2]),
    ]
    for load in loads:
        load.start()

    barrier = pltpu.get_barrier_semaphore()

    @pl.loop(1, bricks)
    def _(k):
        pl.semaphore_signal(
            barrier, inc=1, device_id={"brick": lax.rem(me + k, bricks)}, device_id_type=MESH
        )

    @pl.loop(1, freqs)
    def _(k):
        pl.semaphore_signal(
            barrier, inc=1, device_id={"freq": lax.rem(mine + k, freqs)}, device_id_type=MESH
        )

    target = target_ref[...]
    down = lax.broadcasted_iota(jnp.int32, (held, held), 0)
    across = lax.broadcasted_iota(jnp.int32, (held, held), 1)
    diagonal = down == across
    target_col = jnp.sum(jnp.where(diagonal, target, 0), axis=1, keepdims=True)
    same = target_col == target
    rank = jnp.sum(jnp.where(same & (down < across), 1, 0), axis=0, keepdims=True)
    rank_col = jnp.sum(jnp.where(same & (across < down), 1, 0), axis=1, keepdims=True)
    place = target * SLOTS + rank

    value = receiver_ref[...] + 1
    names = lax.broadcasted_iota(jnp.int32, (bricks, held), 0) == target
    lanes = lax.broadcasted_iota(jnp.int32, (held, 128), 1)
    by_rank = (rank_col == lanes).astype(jnp.float32).astype(jnp.bfloat16)
    high = jnp.where(names, value // 16, 0).astype(jnp.float32).astype(jnp.bfloat16)
    low = jnp.where(names, lax.rem(value, 16), 0).astype(jnp.float32).astype(jnp.bfloat16)
    high = jnp.dot(high, by_rank, preferred_element_type=jnp.float32)
    low = jnp.dot(low, by_rank, preferred_element_type=jnp.float32)
    labels_out[...] = (high * 16.0 + low).astype(jnp.int32)

    def label_copy(other, row):
        return pltpu.make_async_remote_copy(
            src_ref=labels_out.at[pl.ds(other, 1)],
            dst_ref=labels_in.at[pl.ds(row, 1)],
            send_sem=label_send_sem.at[other],
            recv_sem=label_recv_sem.at[row],
            device_id={"brick": other},
            device_id_type=MESH,
        )

    def block_copy(other, row):
        return pltpu.make_async_remote_copy(
            src_ref=outgoing.at[other],
            dst_ref=incoming.at[row],
            send_sem=send_sem.at[other],
            recv_sem=recv_sem.at[row],
            device_id={"brick": other},
            device_id_type=MESH,
        )

    def build(z):
        slots = lax.broadcasted_iota(jnp.int32, (SIDE * SLOTS, held), 0) + z * (SIDE * SLOTS)
        select = (slots == place).astype(jnp.float32).astype(jnp.bfloat16)
        rows = jnp.dot(select, panels[...], preferred_element_type=jnp.float32)
        outgoing[pl.ds(z * SIDE, SIDE)] = rows.reshape(SIDE, SLOTS, width).astype(jnp.bfloat16)

    loads[0].wait()
    build(lax.rem(my_z + zigzag(0), SIDE))
    pl.semaphore_wait(barrier, bricks - 1 + freqs - 1)

    @pl.loop(1, bricks)
    def _(k):
        other = lax.rem(me + k, bricks)
        label_copy(other, me).start()

    @pl.loop(0, SIDE)
    def _(step):
        z = lax.rem(my_z + zigzag(step), SIDE)

        @pl.when(step > 0)
        def _():
            build(z)

        @pl.loop(0, SIDE)
        def _(inner):
            y = lax.rem(my_y + zigzag(inner), SIDE)
            other = z * SIDE + y

            @pl.when(other != me)
            def _():
                block_copy(other, me).start()

    loads[1].wait()
    for k in range(columns_ref.shape[0]):
        for r in range(SIDE):
            tile = jnp.zeros((blocks.shape[2], blocks.shape[3]), jnp.bfloat16)
            for j in range(columns_ref.shape[1]):
                tile = jnp.where(columns_ref[k, j] == r, blocks[k, j], tile)
            dense[0, pl.ds(k * 64, 64), pl.ds(r * 64, 64)] = tile[:, :64]
            dense[1, pl.ds(k * 64, 64), pl.ds(r * 64, 64)] = tile[:, 64:]

    labels_in[pl.ds(me, 1)] = labels_out[pl.ds(me, 1)]

    @pl.loop(1, bricks)
    def _(k):
        other = lax.rem(me + k, bricks)
        label_copy(other, other).wait_recv()

    named = labels_in[...]
    pick = lax.broadcasted_iota(jnp.int32, (bricks, SLOTS, 128), 1) == lax.broadcasted_iota(
        jnp.int32, (bricks, SLOTS, 128), 2
    )
    label = jnp.sum(jnp.where(pick, named[:, None, :], 0), axis=2, keepdims=True)
    label = label.reshape(bricks * SLOTS, 1) - 1
    receivers = lax.broadcasted_iota(jnp.int32, (bricks * SLOTS, dense.shape[2]), 1)
    onehot = (receivers == label).astype(jnp.float32).astype(jnp.bfloat16)
    dims = (((1,), (1,)), ((), ()))
    real = lax.dot_general(onehot, dense[0], dims, preferred_element_type=jnp.float32)
    imag = lax.dot_general(onehot, dense[1], dims, preferred_element_type=jnp.float32)
    left[0, :, pl.ds(0, tx)] = real.astype(jnp.bfloat16)
    left[0, :, pl.ds(tx, tx)] = (-imag).astype(jnp.bfloat16)
    left[1, :, pl.ds(0, tx)] = imag.astype(jnp.bfloat16)
    left[1, :, pl.ds(tx, tx)] = real.astype(jnp.bfloat16)

    loads[2].wait()

    @pl.loop(0, 4)
    def _(tile):
        rows = pl.ds(pl.multiple_of(tile * 128, 128), 128)
        product[0, rows] = jnp.dot(left[0, rows], fields[...], preferred_element_type=jnp.float32)
        product[1, rows] = jnp.dot(left[1, rows], fields[...], preferred_element_type=jnp.float32)

    def term(block, source):
        rows = pl.ds(pl.multiple_of(source * SLOTS, SLOTS), SLOTS)
        block = block.astype(jnp.float32)
        both = product[0, rows] * block[:, :span] - product[1, rows] * block[:, span:]
        return both[:, :cells] + both[:, cells : 2 * cells] + both[:, 2 * cells :]

    total[...] = term(outgoing[me], me)

    @pl.loop(0, SIDE)
    def _(step):
        z = lax.rem(my_z - zigzag(step) + SIDE, SIDE)

        @pl.loop(0, SIDE)
        def _(inner):
            y = lax.rem(my_y - zigzag(inner) + SIDE, SIDE)
            source = z * SIDE + y

            @pl.when(source != me)
            def _():
                block_copy(source, source).wait_recv()
                total[...] += term(incoming[source], source)

    partial[...] = jnp.sum(total[...], axis=0, keepdims=True)

    def sum_copy(other, row):
        return pltpu.make_async_remote_copy(
            src_ref=partial,
            dst_ref=gathered.at[row],
            send_sem=sum_send_sem.at[other],
            recv_sem=sum_recv_sem.at[row],
            device_id={"freq": other},
            device_id_type=MESH,
        )

    @pl.loop(1, freqs)
    def _(k):
        sum_copy(lax.rem(mine + k, freqs), mine).start()

    gathered[mine] = partial[...]

    @pl.loop(1, bricks)
    def _(k):
        other = lax.rem(me + k, bricks)
        label_copy(other, me).wait_send()
        block_copy(other, me).wait_send()

    @pl.loop(1, freqs)
    def _(k):
        other = lax.rem(mine + k, freqs)
        sum_copy(other, other).wait_recv()
        sum_copy(other, mine).wait_send()

    result = gathered[0]
    for row in range(1, freqs):
        result = result + gathered[row]
    out_ref[...] = result


def on_device(
    forward_fields, adjoint_panels, residual_blocks, residual_columns, panel_brick, panel_receiver
):
    bricks, freqs = lax.axis_size("brick"), lax.axis_size("freq")
    held, span = adjoint_panels.shape[1], adjoint_panels.shape[3]
    cells = span // 3
    tx = forward_fields.shape[3]
    panels = adjoint_panels[0].reshape(held, 2 * span)
    fields = forward_fields[0, 0].reshape(2 * tx, span)
    blocks = residual_blocks[0, 0]
    slots = bricks * SLOTS
    any_space = pl.BlockSpec(memory_space=pl.ANY)
    vmem = pl.BlockSpec(memory_space=pltpu.VMEM)
    summed = pl.pallas_call(
        functools.partial(kernel, bricks, freqs),
        out_shape=jax.ShapeDtypeStruct((1, cells), jnp.float32),
        in_specs=[
            pl.BlockSpec(memory_space=pltpu.SMEM), vmem, vmem, any_space, any_space, any_space,
        ],
        out_specs=vmem,
        scratch_shapes=[
            pltpu.VMEM(panels.shape, jnp.bfloat16),
            pltpu.VMEM(fields.shape, jnp.bfloat16),
            pltpu.VMEM(blocks.shape, jnp.bfloat16),
            pltpu.VMEM((bricks, SLOTS, 2 * span), jnp.bfloat16),
            pltpu.VMEM((bricks, SLOTS, 2 * span), jnp.bfloat16),
            pltpu.VMEM((bricks, 128), jnp.int32),
            pltpu.VMEM((bricks, 128), jnp.int32),
            pltpu.VMEM((2, tx, 512), jnp.bfloat16),
            pltpu.VMEM((2, slots, 2 * tx), jnp.bfloat16),
            pltpu.VMEM((2, slots, span), jnp.float32),
            pltpu.VMEM((SLOTS, cells), jnp.float32),
            pltpu.VMEM((1, cells), jnp.float32),
            pltpu.VMEM((freqs, 1, cells), jnp.float32),
            pltpu.SemaphoreType.DMA((3,)),
            pltpu.SemaphoreType.DMA((bricks,)),
            pltpu.SemaphoreType.DMA((bricks,)),
            pltpu.SemaphoreType.DMA((bricks,)),
            pltpu.SemaphoreType.DMA((bricks,)),
            pltpu.SemaphoreType.DMA((freqs,)),
            pltpu.SemaphoreType.DMA((freqs,)),
        ],
        compiler_params=pltpu.CompilerParams(collective_id=0, has_side_effects=True),
        name="exchange_and_correlate",
    )(
        residual_columns[0],
        panel_brick.reshape(1, held),
        panel_receiver.reshape(1, held),
        panels,
        fields,
        blocks,
    )
    share = cells // freqs
    return lax.dynamic_slice_in_dim(summed[0], lax.axis_index("freq") * share, share, 0)


def solution(mesh):
    placed = (
        P("freq", "brick", None, None, None),
        P("freq", "brick", None, None),
        P("freq", "brick", None, None, None, None),
        P("brick", None, None),
        P("brick", None),
        P("brick"),
    )
    return jax.shard_map(
        on_device, mesh=mesh, in_specs=placed, out_specs=P(("brick", "freq")), check_vma=False
    )
```

```python
import functools

import jax
import jax.numpy as jnp
from jax import lax
from jax.experimental import pallas as pl
from jax.experimental.pallas import tpu as pltpu
from jax.sharding import PartitionSpec as P

SIDE = 8
SLOTS = 8
MESH = pl.DeviceIdType.MESH


def zigzag(step):
    half = (step + 1) // 2
    return 4 + half * (1 - 2 * lax.rem(step, 2))


def kernel(
    freqs, columns_ref, target_ref, receiver_ref, panels_hbm, fields_hbm, blocks_hbm,
    out_ref,
    panels, fields, blocks, out_a, out_b, mid_a, mid_b, in_a, in_b, labels_own, labels_mid,
    labels_in, dense, left, product, total, partial, gathered,
    load_sem, label_send1, label_recv1, label_send2, label_recv2,
    send1_a, recv1_a, send1_b, recv1_b, send2_a, recv2_a, send2_b, recv2_b,
    sum_send_sem, sum_recv_sem,
):
    me = lax.axis_index("brick")
    mine = lax.axis_index("freq")
    z, y = me // SIDE, lax.rem(me, SIDE)
    held = panels.shape[0]
    span = fields.shape[1]
    cells = span // 3
    tx = fields.shape[0] // 2

    def remote(src, dst, send, recv, **where):
        return pltpu.make_async_remote_copy(
            src_ref=src, dst_ref=dst, send_sem=send, recv_sem=recv,
            device_id=where, device_id_type=MESH,
        )

    def at(row, column):
        return row * SIDE + column

    def around(here, step):
        return lax.rem(here + zigzag(step), SIDE)

    def back(here, step):
        return lax.rem(here - zigzag(step) + SIDE, SIDE)

    loads = [
        pltpu.make_async_copy(panels_hbm, panels, load_sem.at[0]),
        pltpu.make_async_copy(blocks_hbm, blocks, load_sem.at[1]),
        pltpu.make_async_copy(fields_hbm, fields, load_sem.at[2]),
    ]
    for load in loads:
        load.start()

    barrier = pltpu.get_barrier_semaphore()

    @pl.loop(1, SIDE)
    def _(k):
        other_z, other_y = lax.rem(z + k, SIDE), lax.rem(y + k, SIDE)
        pl.semaphore_signal(
            barrier, inc=1, device_id={"brick": at(other_z, y)}, device_id_type=MESH
        )
        pl.semaphore_signal(
            barrier, inc=1, device_id={"brick": at(z, other_y)}, device_id_type=MESH
        )

    @pl.loop(1, freqs)
    def _(k):
        pl.semaphore_signal(
            barrier, inc=1, device_id={"freq": lax.rem(mine + k, freqs)}, device_id_type=MESH
        )

    target = target_ref[...]
    down = lax.broadcasted_iota(jnp.int32, (held, held), 0)
    across = lax.broadcasted_iota(jnp.int32, (held, held), 1)
    diagonal = down == across
    target_col = jnp.sum(jnp.where(diagonal, target, 0), axis=1, keepdims=True)
    same = target_col == target
    rank = jnp.sum(jnp.where(same & (down < across), 1, 0), axis=0, keepdims=True)
    rank_col = jnp.sum(jnp.where(same & (across < down), 1, 0), axis=1, keepdims=True)
    target_z, target_y = target // SIDE, lax.rem(target, SIDE)
    place_a = target * SLOTS + rank
    place_b = (target_y * SIDE + target_z) * SLOTS + rank

    value = receiver_ref[...] + 1
    names = lax.broadcasted_iota(jnp.int32, (SIDE, held), 0) == target_z
    lanes = lax.broadcasted_iota(jnp.int32, (held, 128), 1)
    by_lane = lax.rem(target_col, SIDE) * SLOTS + rank_col == lanes
    by_lane = by_lane.astype(jnp.float32).astype(jnp.bfloat16)
    high = jnp.where(names, value // 16, 0).astype(jnp.float32).astype(jnp.bfloat16)
    low = jnp.where(names, lax.rem(value, 16), 0).astype(jnp.float32).astype(jnp.bfloat16)
    high = jnp.dot(high, by_lane, preferred_element_type=jnp.float32)
    low = jnp.dot(low, by_lane, preferred_element_type=jnp.float32)
    labels_own[...] = (high * 16.0 + low).astype(jnp.int32)

    def label_copy1(other, row):
        return remote(
            labels_own.at[pl.ds(other, 1)], labels_mid.at[pl.ds(row, 1)],
            label_send1.at[other], label_recv1.at[row], brick=at(other, y),
        )

    def label_copy2(other, row):
        return remote(
            labels_mid, labels_in.at[row],
            label_send2.at[other], label_recv2.at[row], brick=at(z, other),
        )

    def first_a(other, row):
        return remote(
            out_a.at[other], mid_a.at[row], send1_a.at[other], recv1_a.at[row],
            brick=at(other, y),
        )

    def first_b(other, row):
        return remote(
            out_b.at[other], mid_b.at[row], send1_b.at[other], recv1_b.at[row],
            brick=at(z, other),
        )

    def second_a(block, source, other, column):
        index = at(column, source)
        return remote(
            block.at[other], in_a.at[index], send2_a.at[at(source, other)], recv2_a.at[index],
            brick=at(z, other),
        )

    def second_b(block, source, other, row):
        index = at(source, row)
        return remote(
            block.at[other], in_b.at[index], send2_b.at[at(source, other)], recv2_b.at[index],
            brick=at(other, y),
        )

    def build(group, place, part, into):
        slots = lax.broadcasted_iota(jnp.int32, (SIDE * SLOTS, held), 0) + group * (SIDE * SLOTS)
        select = (slots == place).astype(jnp.float32).astype(jnp.bfloat16)
        rows = jnp.dot(
            select, panels[:, part * span : (part + 1) * span],
            preferred_element_type=jnp.float32,
        )
        into[group] = rows.reshape(SIDE, SLOTS, span).astype(jnp.bfloat16)

    loads[0].wait()
    build(around(z, 0), place_a, 0, out_a)
    build(around(y, 0), place_b, 1, out_b)
    pl.semaphore_wait(barrier, 2 * (SIDE - 1) + freqs - 1)

    @pl.loop(1, SIDE)
    def _(k):
        label_copy1(lax.rem(z + k, SIDE), z).start()

    @pl.loop(0, SIDE)
    def _(step):
        other_z, other_y = around(z, step), around(y, step)

        @pl.when(step > 0)
        def _():
            build(other_z, place_a, 0, out_a)
            build(other_y, place_b, 1, out_b)

        @pl.when(step < SIDE - 1)
        def _():
            first_a(other_z, z).start()
            first_b(other_y, y).start()

    @pl.loop(0, SIDE - 1)
    def _(step):
        second_a(out_a.at[z], z, around(y, step), y).start()
        second_b(out_b.at[y], y, around(z, step), z).start()

    labels_mid[pl.ds(z, 1)] = labels_own[pl.ds(z, 1)]

    @pl.loop(1, SIDE)
    def _(k):
        other = lax.rem(z + k, SIDE)
        label_copy1(other, other).wait_recv()

    @pl.loop(1, SIDE)
    def _(k):
        label_copy2(lax.rem(y + k, SIDE), y).start()

    labels_in[y] = labels_mid[...]

    loads[1].wait()
    for k in range(columns_ref.shape[0]):
        for r in range(SIDE):
            tile = jnp.zeros((blocks.shape[2], blocks.shape[3]), jnp.bfloat16)
            for j in range(columns_ref.shape[1]):
                tile = jnp.where(columns_ref[k, j] == r, blocks[k, j], tile)
            dense[0, pl.ds(k * 64, 64), pl.ds(r * 64, 64)] = tile[:, :64]
            dense[1, pl.ds(k * 64, 64), pl.ds(r * 64, 64)] = tile[:, 64:]

    @pl.loop(1, SIDE)
    def _(k):
        other = lax.rem(y + k, SIDE)
        label_copy2(other, other).wait_recv()

    slots = SIDE * SIDE * SLOTS
    named = labels_in[...].reshape(SIDE * SIDE, 128)
    pick = lax.broadcasted_iota(jnp.int32, (SIDE * SIDE, SLOTS, 128), 1) + y * SLOTS
    pick = pick == lax.broadcasted_iota(jnp.int32, (SIDE * SIDE, SLOTS, 128), 2)
    label = jnp.sum(jnp.where(pick, named[:, None, :], 0), axis=2, keepdims=True)
    label = label.reshape(slots, 1) - 1
    receivers = lax.broadcasted_iota(jnp.int32, (slots, dense.shape[2]), 1)
    onehot = (receivers == label).astype(jnp.float32).astype(jnp.bfloat16)
    dims = (((1,), (1,)), ((), ()))
    real = lax.dot_general(onehot, dense[0], dims, preferred_element_type=jnp.float32)
    imag = lax.dot_general(onehot, dense[1], dims, preferred_element_type=jnp.float32)
    left[0, :, pl.ds(0, tx)] = real.astype(jnp.bfloat16)
    left[0, :, pl.ds(tx, tx)] = (-imag).astype(jnp.bfloat16)
    left[1, :, pl.ds(0, tx)] = imag.astype(jnp.bfloat16)
    left[1, :, pl.ds(tx, tx)] = real.astype(jnp.bfloat16)

    loads[2].wait()

    @pl.loop(0, 4)
    def _(tile):
        rows = pl.ds(pl.multiple_of(tile * 128, 128), 128)
        product[0, rows] = jnp.dot(left[0, rows], fields[...], preferred_element_type=jnp.float32)
        product[1, rows] = jnp.dot(left[1, rows], fields[...], preferred_element_type=jnp.float32)

    def term(part, block, index):
        rows = pl.ds(pl.multiple_of(index * SLOTS, SLOTS), SLOTS)
        both = product[part, rows] * block.astype(jnp.float32)
        return both[:, :cells] + both[:, cells : 2 * cells] + both[:, 2 * cells :]

    total[...] = term(0, out_a[z, y], at(y, z)) - term(1, out_b[y, z], at(y, z))

    @pl.loop(0, SIDE - 1)
    def _(step):
        source_z, source_y = back(z, step), back(y, step)
        first_a(source_z, source_z).wait_recv()

        @pl.loop(0, SIDE - 1)
        def _(inner):
            second_a(mid_a.at[source_z], source_z, around(y, inner), y).start()

        first_b(source_y, source_y).wait_recv()

        @pl.loop(0, SIDE - 1)
        def _(inner):
            second_b(mid_b.at[source_y], source_y, around(z, inner), z).start()

        total[...] += term(0, mid_a[source_z, y], at(y, source_z)) - term(
            1, mid_b[source_y, z], at(source_y, z)
        )

    @pl.loop(0, SIDE)
    def _(step):
        source = lax.rem(step + SIDE - 1, SIDE)
        source_z, source_y = back(z, source), back(y, source)

        @pl.loop(0, SIDE - 1)
        def _(inner):
            column, row = back(y, inner), back(z, inner)
            index_a, index_b = at(column, source_z), at(source_y, row)
            second_a(mid_a.at[source_z], source_z, column, column).wait_recv()
            second_b(mid_b.at[source_y], source_y, row, row).wait_recv()
            total[...] += term(0, in_a[index_a], index_a) - term(1, in_b[index_b], index_b)

    partial[...] = jnp.sum(total[...], axis=0, keepdims=True)

    def sum_copy(other, row):
        return remote(
            partial, gathered.at[row], sum_send_sem.at[other], sum_recv_sem.at[row], freq=other
        )

    @pl.loop(1, freqs)
    def _(k):
        sum_copy(lax.rem(mine + k, freqs), mine).start()

    gathered[mine] = partial[...]

    @pl.loop(1, SIDE)
    def _(k):
        other_z, other_y = lax.rem(z + k, SIDE), lax.rem(y + k, SIDE)
        label_copy1(other_z, z).wait_send()
        label_copy2(other_y, y).wait_send()
        first_a(other_z, z).wait_send()
        first_b(other_y, y).wait_send()

        @pl.loop(0, SIDE)
        def _(source):
            second_a(mid_a.at[source], source, other_y, y).wait_send()
            second_b(mid_b.at[source], source, other_z, z).wait_send()

    @pl.loop(1, freqs)
    def _(k):
        other = lax.rem(mine + k, freqs)
        sum_copy(other, other).wait_recv()
        sum_copy(other, mine).wait_send()

    result = gathered[0]
    for row in range(1, freqs):
        result = result + gathered[row]
    out_ref[...] = result


def on_device(
    forward_fields, adjoint_panels, residual_blocks, residual_columns, panel_brick, panel_receiver
):
    bricks, freqs = lax.axis_size("brick"), lax.axis_size("freq")
    held, span = adjoint_panels.shape[1], adjoint_panels.shape[3]
    cells = span // 3
    tx = forward_fields.shape[3]
    panels = adjoint_panels[0].reshape(held, 2 * span)
    fields = forward_fields[0, 0].reshape(2 * tx, span)
    blocks = residual_blocks[0, 0]
    slots = bricks * SLOTS
    half = (SIDE, SIDE, SLOTS, span)
    any_space = pl.BlockSpec(memory_space=pl.ANY)
    vmem = pl.BlockSpec(memory_space=pltpu.VMEM)
    summed = pl.pallas_call(
        functools.partial(kernel, freqs),
        out_shape=jax.ShapeDtypeStruct((1, cells), jnp.float32),
        in_specs=[
            pl.BlockSpec(memory_space=pltpu.SMEM), vmem, vmem, any_space, any_space, any_space,
        ],
        out_specs=vmem,
        scratch_shapes=[
            pltpu.VMEM(panels.shape, jnp.bfloat16),
            pltpu.VMEM(fields.shape, jnp.bfloat16),
            pltpu.VMEM(blocks.shape, jnp.bfloat16),
            pltpu.VMEM(half, jnp.bfloat16),
            pltpu.VMEM(half, jnp.bfloat16),
            pltpu.VMEM(half, jnp.bfloat16),
            pltpu.VMEM(half, jnp.bfloat16),
            pltpu.VMEM((bricks, SLOTS, span), jnp.bfloat16),
            pltpu.VMEM((bricks, SLOTS, span), jnp.bfloat16),
            pltpu.VMEM((SIDE, 128), jnp.int32),
            pltpu.VMEM((SIDE, 128), jnp.int32),
            pltpu.VMEM((SIDE, SIDE, 128), jnp.int32),
            pltpu.VMEM((2, tx, 512), jnp.bfloat16),
            pltpu.VMEM((2, slots, 2 * tx), jnp.bfloat16),
            pltpu.VMEM((2, slots, span), jnp.float32),
            pltpu.VMEM((SLOTS, cells), jnp.float32),
            pltpu.VMEM((1, cells), jnp.float32),
            pltpu.VMEM((freqs, 1, cells), jnp.float32),
            pltpu.SemaphoreType.DMA((3,)),
            *[pltpu.SemaphoreType.DMA((SIDE,))] * 8,
            *[pltpu.SemaphoreType.DMA((bricks,))] * 4,
            pltpu.SemaphoreType.DMA((freqs,)),
            pltpu.SemaphoreType.DMA((freqs,)),
        ],
        compiler_params=pltpu.CompilerParams(collective_id=0, has_side_effects=True),
        name="exchange_and_correlate",
    )(
        residual_columns[0],
        panel_brick.reshape(1, held),
        panel_receiver.reshape(1, held),
        panels,
        fields,
        blocks,
    )
    share = cells // freqs
    return lax.dynamic_slice_in_dim(summed[0], lax.axis_index("freq") * share, share, 0)


def solution(mesh):
    placed = (
        P("freq", "brick", None, None, None),
        P("freq", "brick", None, None),
        P("freq", "brick", None, None, None, None),
        P("brick", None, None),
        P("brick", None),
        P("brick"),
    )
    return jax.shard_map(
        on_device, mesh=mesh, in_specs=placed, out_specs=P(("brick", "freq")), check_vma=False
    )
```

```python
import functools

import jax
import jax.numpy as jnp
from jax import lax
from jax.experimental import pallas as pl
from jax.experimental.pallas import tpu as pltpu
from jax.sharding import PartitionSpec as P

SIDE = 8
SLOTS = 8
MESH = pl.DeviceIdType.MESH


def zigzag(step):
    half = (step + 1) // 2
    return 4 + half * (1 - 2 * lax.rem(step, 2))


def kernel(
    freqs, columns_ref, target_ref, receiver_ref, panels_hbm, fields_hbm, blocks_hbm,
    out_ref,
    stored, panels, fields, blocks, out_a, out_b, mid_a, mid_b, in_a, in_b, labels_own, labels_mid,
    labels_in, dense, left, product, total, partial, gathered,
    load_sem, label_send1, label_recv1, label_send2, label_recv2,
    send1_a, recv1_a, send1_b, recv1_b, send2_a, recv2_a, send2_b, recv2_b,
    sum_send_sem, sum_recv_sem,
):
    me = lax.axis_index("brick")
    mine = lax.axis_index("freq")
    z, y = me // SIDE, lax.rem(me, SIDE)
    held = panels.shape[1]
    span = fields.shape[1]
    cells = span // 3
    tx = fields.shape[0] // 2

    def remote(src, dst, send, recv, **where):
        return pltpu.make_async_remote_copy(
            src_ref=src, dst_ref=dst, send_sem=send, recv_sem=recv,
            device_id=where, device_id_type=MESH,
        )

    def at(row, column):
        return row * SIDE + column

    def around(here, step):
        return lax.rem(here + zigzag(step), SIDE)

    def back(here, step):
        return lax.rem(here - zigzag(step) + SIDE, SIDE)

    loads = [
        pltpu.make_async_copy(panels_hbm, stored, load_sem.at[0]),
        pltpu.make_async_copy(blocks_hbm, blocks, load_sem.at[1]),
        pltpu.make_async_copy(fields_hbm, fields, load_sem.at[2]),
    ]
    for load in loads:
        load.start()

    barrier = pltpu.get_barrier_semaphore()

    @pl.loop(1, SIDE)
    def _(k):
        other_z, other_y = lax.rem(z + k, SIDE), lax.rem(y + k, SIDE)
        pl.semaphore_signal(
            barrier, inc=1, device_id={"brick": at(other_z, y)}, device_id_type=MESH
        )
        pl.semaphore_signal(
            barrier, inc=1, device_id={"brick": at(z, other_y)}, device_id_type=MESH
        )

    @pl.loop(1, freqs)
    def _(k):
        pl.semaphore_signal(
            barrier, inc=1, device_id={"freq": lax.rem(mine + k, freqs)}, device_id_type=MESH
        )

    target = target_ref[...]
    down = lax.broadcasted_iota(jnp.int32, (held, held), 0)
    across = lax.broadcasted_iota(jnp.int32, (held, held), 1)
    diagonal = down == across
    target_col = jnp.sum(jnp.where(diagonal, target, 0), axis=1, keepdims=True)
    same = target_col == target
    rank = jnp.sum(jnp.where(same & (down < across), 1, 0), axis=0, keepdims=True)
    rank_col = jnp.sum(jnp.where(same & (across < down), 1, 0), axis=1, keepdims=True)
    target_z, target_y = target // SIDE, lax.rem(target, SIDE)
    place_a = target * SLOTS + rank
    place_b = (target_y * SIDE + target_z) * SLOTS + rank

    value = receiver_ref[...] + 1
    names = lax.broadcasted_iota(jnp.int32, (SIDE, held), 0) == target_z
    lanes = lax.broadcasted_iota(jnp.int32, (held, 128), 1)
    by_lane = lax.rem(target_col, SIDE) * SLOTS + rank_col == lanes
    by_lane = by_lane.astype(jnp.float32).astype(jnp.bfloat16)
    high = jnp.where(names, value // 16, 0).astype(jnp.float32).astype(jnp.bfloat16)
    low = jnp.where(names, lax.rem(value, 16), 0).astype(jnp.float32).astype(jnp.bfloat16)
    high = jnp.dot(high, by_lane, preferred_element_type=jnp.float32)
    low = jnp.dot(low, by_lane, preferred_element_type=jnp.float32)
    labels_own[...] = (high * 16.0 + low).astype(jnp.int32)

    def label_copy1(other, row):
        return remote(
            labels_own.at[pl.ds(other, 1)], labels_mid.at[pl.ds(row, 1)],
            label_send1.at[other], label_recv1.at[row], brick=at(other, y),
        )

    def label_copy2(other, row):
        return remote(
            labels_mid, labels_in.at[row],
            label_send2.at[other], label_recv2.at[row], brick=at(z, other),
        )

    def first_a(other, row):
        return remote(
            out_a.at[other], mid_a.at[row], send1_a.at[other], recv1_a.at[row],
            brick=at(other, y),
        )

    def first_b(other, row):
        return remote(
            out_b.at[other], mid_b.at[row], send1_b.at[other], recv1_b.at[row],
            brick=at(z, other),
        )

    def second_a(block, source, other, column):
        index = at(column, source)
        return remote(
            block.at[other], in_a.at[index], send2_a.at[at(source, other)], recv2_a.at[index],
            brick=at(z, other),
        )

    def second_b(block, source, other, row):
        index = at(source, row)
        return remote(
            block.at[other], in_b.at[index], send2_b.at[at(source, other)], recv2_b.at[index],
            brick=at(other, y),
        )

    def build(group, place, part, into):
        slots = lax.broadcasted_iota(jnp.int32, (SIDE * SLOTS, held), 0) + group * (SIDE * SLOTS)
        select = (slots == place).astype(jnp.float32).astype(jnp.bfloat16)
        rows = jnp.dot(
            select, panels[part], preferred_element_type=jnp.float32,
        )
        into[group] = rows.reshape(SIDE, SLOTS, span).astype(jnp.bfloat16)

    loads[0].wait()
    panels[...] = jnp.swapaxes(stored[...], 0, 1)
    build(around(z, 0), place_a, 0, out_a)
    build(around(y, 0), place_b, 1, out_b)
    pl.semaphore_wait(barrier, 2 * (SIDE - 1) + freqs - 1)

    @pl.loop(1, SIDE)
    def _(k):
        label_copy1(lax.rem(z + k, SIDE), z).start()

    @pl.loop(0, SIDE)
    def _(step):
        other_z, other_y = around(z, step), around(y, step)

        @pl.when(step > 0)
        def _():
            build(other_z, place_a, 0, out_a)
            build(other_y, place_b, 1, out_b)

        @pl.when(step < SIDE - 1)
        def _():
            first_a(other_z, z).start()
            first_b(other_y, y).start()

    @pl.loop(0, SIDE - 1)
    def _(step):
        second_a(out_a.at[z], z, around(y, step), y).start()
        second_b(out_b.at[y], y, around(z, step), z).start()

    labels_mid[pl.ds(z, 1)] = labels_own[pl.ds(z, 1)]

    @pl.loop(1, SIDE)
    def _(k):
        other = lax.rem(z + k, SIDE)
        label_copy1(other, other).wait_recv()

    @pl.loop(1, SIDE)
    def _(k):
        label_copy2(lax.rem(y + k, SIDE), y).start()

    labels_in[y] = labels_mid[...]

    loads[1].wait()
    for k in range(columns_ref.shape[2]):
        for r in range(SIDE):
            tile = jnp.zeros((blocks.shape[2], blocks.shape[3]), jnp.bfloat16)
            for j in range(columns_ref.shape[0]):
                tile = jnp.where(columns_ref[j, 0, k] == r, blocks[k, j], tile)
            dense[0, pl.ds(k * 64, 64), pl.ds(r * 64, 64)] = tile[:, :64]
            dense[1, pl.ds(k * 64, 64), pl.ds(r * 64, 64)] = tile[:, 64:]

    @pl.loop(1, SIDE)
    def _(k):
        other = lax.rem(y + k, SIDE)
        label_copy2(other, other).wait_recv()

    slots = SIDE * SIDE * SLOTS
    named = labels_in[...].reshape(SIDE * SIDE, 128)
    pick = lax.broadcasted_iota(jnp.int32, (SIDE * SIDE, SLOTS, 128), 1) + y * SLOTS
    pick = pick == lax.broadcasted_iota(jnp.int32, (SIDE * SIDE, SLOTS, 128), 2)
    label = jnp.sum(jnp.where(pick, named[:, None, :], 0), axis=2, keepdims=True)
    label = label.reshape(slots, 1) - 1
    receivers = lax.broadcasted_iota(jnp.int32, (slots, dense.shape[2]), 1)
    onehot = (receivers == label).astype(jnp.float32).astype(jnp.bfloat16)
    dims = (((1,), (1,)), ((), ()))
    real = lax.dot_general(onehot, dense[0], dims, preferred_element_type=jnp.float32)
    imag = lax.dot_general(onehot, dense[1], dims, preferred_element_type=jnp.float32)
    left[0, :, pl.ds(0, tx)] = real.astype(jnp.bfloat16)
    left[0, :, pl.ds(tx, tx)] = (-imag).astype(jnp.bfloat16)
    left[1, :, pl.ds(0, tx)] = imag.astype(jnp.bfloat16)
    left[1, :, pl.ds(tx, tx)] = real.astype(jnp.bfloat16)

    loads[2].wait()

    def multiply(piece):
        part, tile = piece // 4, lax.rem(piece, 4)
        rows = pl.ds(pl.multiple_of(tile * 128, 128), 128)
        product[part, rows] = jnp.dot(
            left[part, rows], fields[...], preferred_element_type=jnp.float32
        )

    def term(part, block, index):
        rows = pl.ds(pl.multiple_of(index * SLOTS, SLOTS), SLOTS)
        both = product[part, rows] * block.astype(jnp.float32)
        return both[:, :cells] + both[:, cells : 2 * cells] + both[:, 2 * cells :]

    @pl.loop(0, SIDE - 1)
    def _(step):
        source_z, source_y = back(z, step), back(y, step)
        first_a(source_z, source_z).wait_recv()

        @pl.loop(0, SIDE - 1)
        def _(inner):
            second_a(mid_a.at[source_z], source_z, around(y, inner), y).start()

        first_b(source_y, source_y).wait_recv()

        @pl.loop(0, SIDE - 1)
        def _(inner):
            second_b(mid_b.at[source_y], source_y, around(z, inner), z).start()

        multiply(step)

    multiply(SIDE - 1)
    total[...] = term(0, out_a[z, y], at(y, z)) - term(1, out_b[y, z], at(y, z))

    @pl.loop(0, SIDE - 1)
    def _(step):
        source_z, source_y = back(z, step), back(y, step)
        total[...] += term(0, mid_a[source_z, y], at(y, source_z)) - term(
            1, mid_b[source_y, z], at(source_y, z)
        )

    @pl.loop(0, SIDE)
    def _(step):
        source = lax.rem(step + SIDE - 1, SIDE)
        source_z, source_y = back(z, source), back(y, source)

        @pl.loop(0, SIDE - 1)
        def _(inner):
            column, row = back(y, inner), back(z, inner)
            index_a, index_b = at(column, source_z), at(source_y, row)
            second_a(mid_a.at[source_z], source_z, column, column).wait_recv()
            second_b(mid_b.at[source_y], source_y, row, row).wait_recv()
            total[...] += term(0, in_a[index_a], index_a) - term(1, in_b[index_b], index_b)

    partial[...] = jnp.sum(total[...], axis=0, keepdims=True)

    def sum_copy(other, row):
        return remote(
            partial, gathered.at[row], sum_send_sem.at[other], sum_recv_sem.at[row], freq=other
        )

    @pl.loop(1, freqs)
    def _(k):
        sum_copy(lax.rem(mine + k, freqs), mine).start()

    gathered[mine] = partial[...]

    @pl.loop(1, SIDE)
    def _(k):
        other_z, other_y = lax.rem(z + k, SIDE), lax.rem(y + k, SIDE)
        label_copy1(other_z, z).wait_send()
        label_copy2(other_y, y).wait_send()
        first_a(other_z, z).wait_send()
        first_b(other_y, y).wait_send()

        @pl.loop(0, SIDE)
        def _(source):
            second_a(mid_a.at[source], source, other_y, y).wait_send()
            second_b(mid_b.at[source], source, other_z, z).wait_send()

    @pl.loop(1, freqs)
    def _(k):
        other = lax.rem(mine + k, freqs)
        sum_copy(other, other).wait_recv()
        sum_copy(other, mine).wait_send()

    result = gathered[0]
    for row in range(1, freqs):
        result = result + gathered[row]
    out_ref[...] = result


def on_device(
    forward_fields, adjoint_panels, residual_blocks, residual_columns, panel_brick, panel_receiver
):
    bricks, freqs = lax.axis_size("brick"), lax.axis_size("freq")
    held, span = adjoint_panels.shape[1], adjoint_panels.shape[3]
    cells = span // 3
    tx = forward_fields.shape[3]
    fields = forward_fields[0, 0].reshape(2 * tx, span)
    blocks = residual_blocks[0, 0]
    slots = bricks * SLOTS
    half = (SIDE, SIDE, SLOTS, span)
    any_space = pl.BlockSpec(memory_space=pl.ANY)
    vmem = pl.BlockSpec(memory_space=pltpu.VMEM)
    summed = pl.pallas_call(
        functools.partial(kernel, freqs),
        out_shape=jax.ShapeDtypeStruct((1, cells), jnp.float32),
        in_specs=[
            pl.BlockSpec(memory_space=pltpu.SMEM), vmem, vmem, any_space, any_space, any_space,
        ],
        out_specs=vmem,
        scratch_shapes=[
            pltpu.VMEM((held, 2, span), jnp.bfloat16),
            pltpu.VMEM((2, held, span), jnp.bfloat16),
            pltpu.VMEM(fields.shape, jnp.bfloat16),
            pltpu.VMEM(blocks.shape, jnp.bfloat16),
            pltpu.VMEM(half, jnp.bfloat16),
            pltpu.VMEM(half, jnp.bfloat16),
            pltpu.VMEM(half, jnp.bfloat16),
            pltpu.VMEM(half, jnp.bfloat16),
            pltpu.VMEM((bricks, SLOTS, span), jnp.bfloat16),
            pltpu.VMEM((bricks, SLOTS, span), jnp.bfloat16),
            pltpu.VMEM((SIDE, 128), jnp.int32),
            pltpu.VMEM((SIDE, 128), jnp.int32),
            pltpu.VMEM((SIDE, SIDE, 128), jnp.int32),
            pltpu.VMEM((2, tx, 512), jnp.bfloat16),
            pltpu.VMEM((2, slots, 2 * tx), jnp.bfloat16),
            pltpu.VMEM((2, slots, span), jnp.float32),
            pltpu.VMEM((SLOTS, cells), jnp.float32),
            pltpu.VMEM((1, cells), jnp.float32),
            pltpu.VMEM((freqs, 1, cells), jnp.float32),
            pltpu.SemaphoreType.DMA((3,)),
            *[pltpu.SemaphoreType.DMA((SIDE,))] * 8,
            *[pltpu.SemaphoreType.DMA((bricks,))] * 4,
            pltpu.SemaphoreType.DMA((freqs,)),
            pltpu.SemaphoreType.DMA((freqs,)),
        ],
        compiler_params=pltpu.CompilerParams(collective_id=0, has_side_effects=True),
        name="exchange_and_correlate",
    )(
        residual_columns.transpose(2, 0, 1),
        panel_brick.reshape(1, held),
        panel_receiver.reshape(1, held),
        adjoint_panels[0],
        fields,
        blocks,
    )
    share = cells // freqs
    return lax.dynamic_slice_in_dim(summed[0], lax.axis_index("freq") * share, share, 0)


def solution(mesh):
    placed = (
        P("freq", "brick", None, None, None),
        P("freq", "brick", None, None),
        P("freq", "brick", None, None, None, None),
        P("brick", None, None),
        P("brick", None),
        P("brick"),
    )
    return jax.shard_map(
        on_device, mesh=mesh, in_specs=placed, out_specs=P(("brick", "freq")), check_vma=False
    )
```

```python
import functools

import jax
import jax.numpy as jnp
from jax import lax
from jax.experimental import pallas as pl
from jax.experimental.pallas import tpu as pltpu
from jax.sharding import PartitionSpec as P

SIDE = 8
SLOTS = 8
MESH = pl.DeviceIdType.MESH
CAPS = (128, 112, 80, 48)
EDGES = (0, 48, 80, 112, 128)
STEPS = len(CAPS)
START_LANE, SPLIT_LANE, FLAG_LANE = 64, 65, 127


def zigzag(step):
    half = (step + 1) // 2
    return 4 + half * (1 - 2 * lax.rem(step, 2))


def padded_kernel(
    freqs, columns_ref, target_ref, receiver_ref, panels_hbm, fields_hbm, blocks_hbm,
    out_ref,
    stored, panels, fields, blocks, out_a, out_b, mid_a, mid_b, in_a, in_b, labels_own, labels_mid,
    labels_in, dense, left, product, total, partial, gathered,
    load_sem, label_send1, label_recv1, label_send2, label_recv2,
    send1_a, recv1_a, send1_b, recv1_b, send2_a, recv2_a, send2_b, recv2_b,
    sum_send_sem, sum_recv_sem,
):
    me = lax.axis_index("brick")
    mine = lax.axis_index("freq")
    z, y = me // SIDE, lax.rem(me, SIDE)
    held = panels.shape[1]
    span = fields.shape[1]
    cells = span // 3
    tx = fields.shape[0] // 2

    def remote(src, dst, send, recv, **where):
        return pltpu.make_async_remote_copy(
            src_ref=src, dst_ref=dst, send_sem=send, recv_sem=recv,
            device_id=where, device_id_type=MESH,
        )

    def at(row, column):
        return row * SIDE + column

    def around(here, step):
        return lax.rem(here + zigzag(step), SIDE)

    def back(here, step):
        return lax.rem(here - zigzag(step) + SIDE, SIDE)

    loads = [
        pltpu.make_async_copy(panels_hbm, stored, load_sem.at[0]),
        pltpu.make_async_copy(blocks_hbm, blocks, load_sem.at[1]),
        pltpu.make_async_copy(fields_hbm, fields, load_sem.at[2]),
    ]
    for load in loads:
        load.start()

    barrier = pltpu.get_barrier_semaphore()

    @pl.loop(1, SIDE)
    def _(k):
        other_z, other_y = lax.rem(z + k, SIDE), lax.rem(y + k, SIDE)
        pl.semaphore_signal(
            barrier, inc=1, device_id={"brick": at(other_z, y)}, device_id_type=MESH
        )
        pl.semaphore_signal(
            barrier, inc=1, device_id={"brick": at(z, other_y)}, device_id_type=MESH
        )

    @pl.loop(1, freqs)
    def _(k):
        pl.semaphore_signal(
            barrier, inc=1, device_id={"freq": lax.rem(mine + k, freqs)}, device_id_type=MESH
        )

    target = target_ref[...]
    down = lax.broadcasted_iota(jnp.int32, (held, held), 0)
    across = lax.broadcasted_iota(jnp.int32, (held, held), 1)
    diagonal = down == across
    target_col = jnp.sum(jnp.where(diagonal, target, 0), axis=1, keepdims=True)
    same = target_col == target
    rank = jnp.sum(jnp.where(same & (down < across), 1, 0), axis=0, keepdims=True)
    rank_col = jnp.sum(jnp.where(same & (across < down), 1, 0), axis=1, keepdims=True)
    target_z, target_y = target // SIDE, lax.rem(target, SIDE)
    place_a = target * SLOTS + rank
    place_b = (target_y * SIDE + target_z) * SLOTS + rank

    value = receiver_ref[...] + 1
    names = lax.broadcasted_iota(jnp.int32, (SIDE, held), 0) == target_z
    lanes = lax.broadcasted_iota(jnp.int32, (held, 128), 1)
    by_lane = lax.rem(target_col, SIDE) * SLOTS + rank_col == lanes
    by_lane = by_lane.astype(jnp.float32).astype(jnp.bfloat16)
    high = jnp.where(names, value // 16, 0).astype(jnp.float32).astype(jnp.bfloat16)
    low = jnp.where(names, lax.rem(value, 16), 0).astype(jnp.float32).astype(jnp.bfloat16)
    high = jnp.dot(high, by_lane, preferred_element_type=jnp.float32)
    low = jnp.dot(low, by_lane, preferred_element_type=jnp.float32)
    labels_own[...] = (high * 16.0 + low).astype(jnp.int32)

    def label_copy1(other, row):
        return remote(
            labels_own.at[pl.ds(other, 1)], labels_mid.at[pl.ds(row, 1)],
            label_send1.at[other], label_recv1.at[row], brick=at(other, y),
        )

    def label_copy2(other, row):
        return remote(
            labels_mid, labels_in.at[row],
            label_send2.at[other], label_recv2.at[row], brick=at(z, other),
        )

    def first_a(other, row):
        return remote(
            out_a.at[other], mid_a.at[row], send1_a.at[other], recv1_a.at[row],
            brick=at(other, y),
        )

    def first_b(other, row):
        return remote(
            out_b.at[other], mid_b.at[row], send1_b.at[other], recv1_b.at[row],
            brick=at(z, other),
        )

    def second_a(block, source, other, column):
        index = at(column, source)
        return remote(
            block.at[other], in_a.at[index], send2_a.at[at(source, other)], recv2_a.at[index],
            brick=at(z, other),
        )

    def second_b(block, source, other, row):
        index = at(source, row)
        return remote(
            block.at[other], in_b.at[index], send2_b.at[at(source, other)], recv2_b.at[index],
            brick=at(other, y),
        )

    def build(group, place, part, into):
        slots = lax.broadcasted_iota(jnp.int32, (SIDE * SLOTS, held), 0) + group * (SIDE * SLOTS)
        select = (slots == place).astype(jnp.float32).astype(jnp.bfloat16)
        rows = jnp.dot(
            select, panels[part], preferred_element_type=jnp.float32,
        )
        into[group] = rows.reshape(SIDE, SLOTS, span).astype(jnp.bfloat16)

    loads[0].wait()
    panels[...] = jnp.swapaxes(stored[...], 0, 1)
    build(around(z, 0), place_a, 0, out_a)
    build(around(y, 0), place_b, 1, out_b)
    pl.semaphore_wait(barrier, 2 * (SIDE - 1) + freqs - 1)

    @pl.loop(1, SIDE)
    def _(k):
        label_copy1(lax.rem(z + k, SIDE), z).start()

    @pl.loop(0, SIDE)
    def _(step):
        other_z, other_y = around(z, step), around(y, step)

        @pl.when(step > 0)
        def _():
            build(other_z, place_a, 0, out_a)
            build(other_y, place_b, 1, out_b)

        @pl.when(step < SIDE - 1)
        def _():
            first_a(other_z, z).start()
            first_b(other_y, y).start()

    @pl.loop(0, SIDE - 1)
    def _(step):
        second_a(out_a.at[z], z, around(y, step), y).start()
        second_b(out_b.at[y], y, around(z, step), z).start()

    labels_mid[pl.ds(z, 1)] = labels_own[pl.ds(z, 1)]

    @pl.loop(1, SIDE)
    def _(k):
        other = lax.rem(z + k, SIDE)
        label_copy1(other, other).wait_recv()

    @pl.loop(1, SIDE)
    def _(k):
        label_copy2(lax.rem(y + k, SIDE), y).start()

    labels_in[y] = labels_mid[...]

    loads[1].wait()
    for k in range(columns_ref.shape[2]):
        for r in range(SIDE):
            tile = jnp.zeros((blocks.shape[2], blocks.shape[3]), jnp.bfloat16)
            for j in range(columns_ref.shape[0]):
                tile = jnp.where(columns_ref[j, 0, k] == r, blocks[k, j], tile)
            dense[0, pl.ds(k * 64, 64), pl.ds(r * 64, 64)] = tile[:, :64]
            dense[1, pl.ds(k * 64, 64), pl.ds(r * 64, 64)] = tile[:, 64:]

    @pl.loop(1, SIDE)
    def _(k):
        other = lax.rem(y + k, SIDE)
        label_copy2(other, other).wait_recv()

    slots = SIDE * SIDE * SLOTS
    named = labels_in[...].reshape(SIDE * SIDE, 128)
    pick = lax.broadcasted_iota(jnp.int32, (SIDE * SIDE, SLOTS, 128), 1) + y * SLOTS
    pick = pick == lax.broadcasted_iota(jnp.int32, (SIDE * SIDE, SLOTS, 128), 2)
    label = jnp.sum(jnp.where(pick, named[:, None, :], 0), axis=2, keepdims=True)
    label = label.reshape(slots, 1) - 1
    receivers = lax.broadcasted_iota(jnp.int32, (slots, dense.shape[2]), 1)
    onehot = (receivers == label).astype(jnp.float32).astype(jnp.bfloat16)
    dims = (((1,), (1,)), ((), ()))
    real = lax.dot_general(onehot, dense[0], dims, preferred_element_type=jnp.float32)
    imag = lax.dot_general(onehot, dense[1], dims, preferred_element_type=jnp.float32)
    left[0, :, pl.ds(0, tx)] = real.astype(jnp.bfloat16)
    left[0, :, pl.ds(tx, tx)] = (-imag).astype(jnp.bfloat16)
    left[1, :, pl.ds(0, tx)] = imag.astype(jnp.bfloat16)
    left[1, :, pl.ds(tx, tx)] = real.astype(jnp.bfloat16)

    loads[2].wait()

    def multiply(piece):
        part, tile = piece // 4, lax.rem(piece, 4)
        rows = pl.ds(pl.multiple_of(tile * 128, 128), 128)
        product[part, rows] = jnp.dot(
            left[part, rows], fields[...], preferred_element_type=jnp.float32
        )

    def term(part, block, index):
        rows = pl.ds(pl.multiple_of(index * SLOTS, SLOTS), SLOTS)
        both = product[part, rows] * block.astype(jnp.float32)
        return both[:, :cells] + both[:, cells : 2 * cells] + both[:, 2 * cells :]

    @pl.loop(0, SIDE - 1)
    def _(step):
        source_z, source_y = back(z, step), back(y, step)
        first_a(source_z, source_z).wait_recv()

        @pl.loop(0, SIDE - 1)
        def _(inner):
            second_a(mid_a.at[source_z], source_z, around(y, inner), y).start()

        first_b(source_y, source_y).wait_recv()

        @pl.loop(0, SIDE - 1)
        def _(inner):
            second_b(mid_b.at[source_y], source_y, around(z, inner), z).start()

        multiply(step)

    multiply(SIDE - 1)
    total[...] = term(0, out_a[z, y], at(y, z)) - term(1, out_b[y, z], at(y, z))

    @pl.loop(0, SIDE - 1)
    def _(step):
        source_z, source_y = back(z, step), back(y, step)
        total[...] += term(0, mid_a[source_z, y], at(y, source_z)) - term(
            1, mid_b[source_y, z], at(source_y, z)
        )

    @pl.loop(0, SIDE)
    def _(step):
        source = lax.rem(step + SIDE - 1, SIDE)
        source_z, source_y = back(z, source), back(y, source)

        @pl.loop(0, SIDE - 1)
        def _(inner):
            column, row = back(y, inner), back(z, inner)
            index_a, index_b = at(column, source_z), at(source_y, row)
            second_a(mid_a.at[source_z], source_z, column, column).wait_recv()
            second_b(mid_b.at[source_y], source_y, row, row).wait_recv()
            total[...] += term(0, in_a[index_a], index_a) - term(1, in_b[index_b], index_b)

    partial[...] = jnp.sum(total[...], axis=0, keepdims=True)

    def sum_copy(other, row):
        return remote(
            partial, gathered.at[row], sum_send_sem.at[other], sum_recv_sem.at[row], freq=other
        )

    @pl.loop(1, freqs)
    def _(k):
        sum_copy(lax.rem(mine + k, freqs), mine).start()

    gathered[mine] = partial[...]

    @pl.loop(1, SIDE)
    def _(k):
        other_z, other_y = lax.rem(z + k, SIDE), lax.rem(y + k, SIDE)
        label_copy1(other_z, z).wait_send()
        label_copy2(other_y, y).wait_send()
        first_a(other_z, z).wait_send()
        first_b(other_y, y).wait_send()

        @pl.loop(0, SIDE)
        def _(source):
            second_a(mid_a.at[source], source, other_y, y).wait_send()
            second_b(mid_b.at[source], source, other_z, z).wait_send()

    @pl.loop(1, freqs)
    def _(k):
        other = lax.rem(mine + k, freqs)
        sum_copy(other, other).wait_recv()
        sum_copy(other, mine).wait_send()

    result = gathered[0]
    for row in range(1, freqs):
        result = result + gathered[row]
    out_ref[...] = result


def count(mask, axis):
    return jnp.sum(jnp.where(mask, 1, 0), axis=axis, keepdims=True)


def iota(shape, axis):
    return lax.broadcasted_iota(jnp.int32, shape, axis)


def onehot(mask):
    return mask.astype(jnp.float32).astype(jnp.bfloat16)


def make_lists(axis_row, axis_col, slot_row, slot_col, here):
    off_row = lax.rem(axis_row - here + SIDE, SIDE)
    off_col = lax.rem(axis_col - here + SIDE, SIDE)
    half = SIDE // 2
    far_row, far_col = off_row == half, off_col == half
    index_row = count(far_col & (slot_col < slot_row), 0)
    index_col = count(far_row & (slot_row < slot_col), 1)
    number = count(far_row, 1)
    up = count((off_row >= 1) & (off_row < half), 1)
    down = count(off_row > half, 1)
    split = jnp.minimum(jnp.maximum(down + number - up, 0) // 2, number)

    def which(off, index):
        plus = ((off >= 1) & (off < half)) | ((off == half) & (index < split))
        minus = (off > half) | ((off == half) & (index >= split))
        return jnp.where(plus, 0, jnp.where(minus, 1, 2))

    list_row, list_col = which(off_row, index_row), which(off_col, index_col)
    dist_row = jnp.minimum(off_row, SIDE - off_row)
    dist_col = jnp.minimum(off_col, SIDE - off_col)
    key_row = (half - dist_row) * (SIDE * SLOTS) + slot_row
    key_col = (half - dist_col) * (SIDE * SLOTS) + slot_col
    place = count((list_col == list_row) & (key_col < key_row), 0)

    over = jnp.zeros((1, 1), jnp.int32)
    for one in range(2):
        for step in range(STEPS):
            length = count((list_row == one) & (dist_row > step), 1)
            over = jnp.maximum(over, jnp.where(length > CAPS[step], 1, 0))

    row = lax.rem(iota((SIDE, 1), 0) - here + SIDE, SIDE)
    row_list = jnp.where(row < half, 0, 1)
    row_dist = jnp.minimum(row, SIDE - row)
    start = count((list_row == row_list) & (dist_row > row_dist), 1)
    return list_row, place, start, split, over


def compact_kernel(
    freqs, columns_ref, target_ref, receiver_ref, panels_hbm, fields_hbm, blocks_hbm,
    out_ref, flag_ref,
    stored, panels, fields, blocks, lists, ring1, ring2, ring3, ring4, mid_a, mid_b, in_a, in_b,
    labels_own, labels_mid, labels_in, dense, left, product, total, partial, gathered,
    load_sem, label_send1, label_recv1, label_send2, label_recv2, hop_send, hop_recv,
    send2_a, recv2_a, send2_b, recv2_b, sum_send_sem, sum_recv_sem,
):
    me = lax.axis_index("brick")
    mine = lax.axis_index("freq")
    z, y = me // SIDE, lax.rem(me, SIDE)
    here = (z, y)
    rings = (ring1, ring2, ring3, ring4)
    mids = (mid_a, mid_b)
    held = panels.shape[1]
    span = fields.shape[1]
    cells = span // 3
    tx = fields.shape[0] // 2
    group = SIDE * SLOTS

    def remote(src, dst, send, recv, **where):
        return pltpu.make_async_remote_copy(
            src_ref=src, dst_ref=dst, send_sem=send, recv_sem=recv,
            device_id=where, device_id_type=MESH,
        )

    def at(row, column):
        return row * SIDE + column

    def along(path, other):
        return at(other, y) if path == 0 else at(z, other)

    def around(start, step):
        return lax.rem(start + zigzag(step), SIDE)

    def back(start, step):
        return lax.rem(start - zigzag(step) + SIDE, SIDE)

    loads = [
        pltpu.make_async_copy(panels_hbm, stored, load_sem.at[0]),
        pltpu.make_async_copy(blocks_hbm, blocks, load_sem.at[1]),
        pltpu.make_async_copy(fields_hbm, fields, load_sem.at[2]),
    ]
    for load in loads:
        load.start()

    barrier = pltpu.get_barrier_semaphore()

    @pl.loop(1, SIDE)
    def _(k):
        for path in range(2):
            other = lax.rem(here[path] + k, SIDE)
            pl.semaphore_signal(
                barrier, inc=1, device_id={"brick": along(path, other)}, device_id_type=MESH
            )

    @pl.loop(1, freqs)
    def _(k):
        pl.semaphore_signal(
            barrier, inc=1, device_id={"freq": lax.rem(mine + k, freqs)}, device_id_type=MESH
        )

    target = target_ref[...]
    down, across = iota((held, held), 0), iota((held, held), 1)
    target_col = jnp.sum(jnp.where(down == across, target, 0), axis=1, keepdims=True)
    same = target_col == target
    rank, rank_col = count(same & (down < across), 0), count(same & (across < down), 1)
    axis_row = (target // SIDE, lax.rem(target, SIDE))
    axis_col = (target_col // SIDE, lax.rem(target_col, SIDE))
    slot_row = tuple(axis_row[1 - path] * SLOTS + rank for path in range(2))
    slot_col = tuple(axis_col[1 - path] * SLOTS + rank_col for path in range(2))

    loads[0].wait()
    panels[...] = jnp.swapaxes(stored[...], 0, 1)
    value = receiver_ref[...] + 1
    over = jnp.zeros((1, 1), jnp.int32)
    lanes = iota((SIDE, 128), 1)
    rows = []
    for path in range(2):
        list_row, place, start, split, too_long = make_lists(
            axis_row[path], axis_col[path], slot_row[path], slot_col[path], here[path]
        )
        over = jnp.maximum(over, too_long)
        for one in range(2):
            select = onehot((iota((CAPS[0], held), 0) == place) & (list_row == one))
            lists[2 * path + one] = jnp.dot(
                select, panels[path], preferred_element_type=jnp.float32
            ).astype(jnp.bfloat16)
        names = iota((SIDE, held), 0) == axis_row[path]
        by_lane = onehot(slot_col[path] == iota((held, 128), 1))
        high = jnp.where(names, value // 16, 0).astype(jnp.float32).astype(jnp.bfloat16)
        low = jnp.where(names, lax.rem(value, 16), 0).astype(jnp.float32).astype(jnp.bfloat16)
        high = jnp.dot(high, by_lane, preferred_element_type=jnp.float32)
        low = jnp.dot(low, by_lane, preferred_element_type=jnp.float32)
        named = (high * 16.0 + low).astype(jnp.int32)
        named = jnp.where(lanes == START_LANE, start, named)
        rows.append(jnp.where(lanes == SPLIT_LANE, split, named))
    labels_own[0] = jnp.where(lanes == FLAG_LANE, over, rows[0])
    labels_own[1] = rows[1]

    def label_copy1(path, other, row):
        return remote(
            labels_own.at[path, pl.ds(other, 1)], labels_mid.at[path, pl.ds(row, 1)],
            label_send1.at[path, other], label_recv1.at[path, row],
            brick=along(path, other),
        )

    def label_copy2(other, row):
        return remote(
            labels_mid.at[0], labels_in.at[row],
            label_send2.at[other], label_recv2.at[row], brick=at(z, other),
        )

    def hop(path, one, step, chunk):
        part = 2 * path + one
        piece = pl.ds(EDGES[chunk], EDGES[chunk + 1] - EDGES[chunk])
        source = lists if step == 0 else rings[step - 1]
        index = (part * STEPS + step) * STEPS + chunk
        other = lax.rem(here[path] + (1 if one == 0 else SIDE - 1), SIDE)
        return remote(
            source.at[part, piece], rings[step].at[part, piece],
            hop_send.at[index], hop_recv.at[index], brick=along(path, other),
        )

    ways = [(path, one) for path in range(2) for one in range(2)]

    def second_a(source, other, column):
        index = at(column, source)
        return remote(
            mid_a.at[source, other], in_a.at[index],
            send2_a.at[at(source, other)], recv2_a.at[index], brick=at(z, other),
        )

    def second_b(source, other, row):
        index = at(source, row)
        return remote(
            mid_b.at[source, other], in_b.at[index],
            send2_b.at[at(source, other)], recv2_b.at[index], brick=at(other, y),
        )

    def pass_on(path, source):
        @pl.loop(0, SIDE - 1)
        def _(inner):
            if path == 0:
                second_a(source, around(y, inner), y).start()
            else:
                second_b(source, around(z, inner), z).start()

    def spread(path, step, one):
        source = lax.rem(here[path] + (SIDE - step - 1 if one == 0 else step + 1), SIDE)
        row = labels_mid[path, pl.ds(source, 1)]
        lane, slot = iota((group, 128), 1), iota((group, 128), 0)
        filled = row > 0
        full = count((lane == slot) & filled, 1) > 0
        index = count((lane < slot) & filled, 1)
        single = iota((1, 128), 1)
        if step < STEPS - 1:
            index = index + jnp.sum(jnp.where(single == START_LANE, row, 0), axis=1, keepdims=True)
        else:
            split = jnp.sum(jnp.where(single == SPLIT_LANE, row, 0), axis=1, keepdims=True)
            if one == 0:
                full = full & (index < split)
            else:
                full = full & (index >= split)
                index = index - split
        select = onehot((iota((group, CAPS[step]), 1) == index) & full)
        return source, jnp.dot(
            select, rings[step][2 * path + one], preferred_element_type=jnp.float32
        )

    def put(path, source, found):
        mids[path][source] = found.reshape(SIDE, SLOTS, span).astype(jnp.bfloat16)

    def deliver(step):
        for path in range(2):
            if step < STEPS - 1:
                for one in range(2):
                    source, found = spread(path, step, one)
                    put(path, source, found)
                    pass_on(path, source)
            else:
                source, found = spread(path, step, 0)
                put(path, source, found + spread(path, step, 1)[1])
                pass_on(path, source)

    def receive(step):
        for chunk in range(STEPS - step):
            for path, one in ways:
                hop(path, one, step, chunk).wait_recv()
                if chunk < STEPS - step - 1:
                    hop(path, one, step + 1, chunk).start()

    pl.semaphore_wait(barrier, 2 * (SIDE - 1) + freqs - 1)

    @pl.loop(1, SIDE)
    def _(k):
        for path in range(2):
            label_copy1(path, lax.rem(here[path] + k, SIDE), here[path]).start()

    for chunk in range(STEPS):
        for path, one in ways:
            hop(path, one, 0, chunk).start()

    for path in range(2):
        select = onehot((iota((group, held), 0) == slot_row[path]) & (axis_row[path] == here[path]))
        put(path, here[path], jnp.dot(select, panels[path], preferred_element_type=jnp.float32))
        labels_mid[path, pl.ds(here[path], 1)] = labels_own[path, pl.ds(here[path], 1)]

    @pl.loop(1, SIDE)
    def _(k):
        for path in range(2):
            other = lax.rem(here[path] + k, SIDE)
            label_copy1(path, other, other).wait_recv()

    @pl.loop(1, SIDE)
    def _(k):
        label_copy2(lax.rem(y + k, SIDE), y).start()

    labels_in[y] = labels_mid[0]

    receive(0)
    for path in range(2):
        pass_on(path, here[path])
    deliver(0)

    loads[1].wait()
    for k in range(columns_ref.shape[2]):
        for r in range(SIDE):
            tile = jnp.zeros((blocks.shape[2], blocks.shape[3]), jnp.bfloat16)
            for j in range(columns_ref.shape[0]):
                tile = jnp.where(columns_ref[j, 0, k] == r, blocks[k, j], tile)
            dense[0, pl.ds(k * 64, 64), pl.ds(r * 64, 64)] = tile[:, :64]
            dense[1, pl.ds(k * 64, 64), pl.ds(r * 64, 64)] = tile[:, 64:]

    receive(1)
    deliver(1)

    @pl.loop(1, SIDE)
    def _(k):
        other = lax.rem(y + k, SIDE)
        label_copy2(other, other).wait_recv()

    slots = SIDE * group
    named = labels_in[...].reshape(SIDE * SIDE, 128)
    flags = jnp.where(iota((SIDE * SIDE, 128), 1) == FLAG_LANE, named, 0)
    flag = jnp.max(jnp.max(flags, axis=1, keepdims=True), axis=0, keepdims=True)
    flag_ref[...] = jnp.broadcast_to(flag, flag_ref.shape)
    pick = iota((SIDE * SIDE, SLOTS, 128), 1) + y * SLOTS == iota((SIDE * SIDE, SLOTS, 128), 2)
    label = jnp.sum(jnp.where(pick, named[:, None, :], 0), axis=2, keepdims=True)
    label = label.reshape(slots, 1) - 1
    chosen = onehot(iota((slots, dense.shape[2]), 1) == label)
    dims = (((1,), (1,)), ((), ()))
    real = lax.dot_general(chosen, dense[0], dims, preferred_element_type=jnp.float32)
    imag = lax.dot_general(chosen, dense[1], dims, preferred_element_type=jnp.float32)
    left[0, :, pl.ds(0, tx)] = real.astype(jnp.bfloat16)
    left[0, :, pl.ds(tx, tx)] = (-imag).astype(jnp.bfloat16)
    left[1, :, pl.ds(0, tx)] = imag.astype(jnp.bfloat16)
    left[1, :, pl.ds(tx, tx)] = real.astype(jnp.bfloat16)

    receive(2)
    deliver(2)
    receive(3)
    deliver(3)

    loads[2].wait()

    @pl.loop(0, SIDE)
    def _(piece):
        part, tile = piece // 4, lax.rem(piece, 4)
        rows = pl.ds(pl.multiple_of(tile * 128, 128), 128)
        product[part, rows] = jnp.dot(
            left[part, rows], fields[...], preferred_element_type=jnp.float32
        )

    def term(part, block, index):
        rows = pl.ds(pl.multiple_of(index * SLOTS, SLOTS), SLOTS)
        both = product[part, rows] * block.astype(jnp.float32)
        return both[:, :cells] + both[:, cells : 2 * cells] + both[:, 2 * cells :]

    total[...] = jnp.zeros_like(total)

    @pl.loop(0, SIDE)
    def _(source):
        total[...] += term(0, mid_a[source, y], at(y, source)) - term(
            1, mid_b[source, z], at(source, z)
        )

    @pl.loop(0, SIDE)
    def _(step):
        source_z, source_y = back(z, SIDE - 1 - step), back(y, SIDE - 1 - step)

        @pl.loop(0, SIDE - 1)
        def _(inner):
            column, row = back(y, inner), back(z, inner)
            index_a, index_b = at(column, source_z), at(source_y, row)
            second_a(source_z, column, column).wait_recv()
            second_b(source_y, row, row).wait_recv()
            total[...] += term(0, in_a[index_a], index_a) - term(1, in_b[index_b], index_b)

    partial[...] = jnp.sum(total[...], axis=0, keepdims=True)

    def sum_copy(other, row):
        return remote(
            partial, gathered.at[row], sum_send_sem.at[other], sum_recv_sem.at[row], freq=other
        )

    @pl.loop(1, freqs)
    def _(k):
        sum_copy(lax.rem(mine + k, freqs), mine).start()

    gathered[mine] = partial[...]

    for step in range(STEPS):
        for chunk in range(STEPS - step):
            for path, one in ways:
                hop(path, one, step, chunk).wait_send()

    @pl.loop(1, SIDE)
    def _(k):
        other_z, other_y = lax.rem(z + k, SIDE), lax.rem(y + k, SIDE)
        label_copy1(0, other_z, z).wait_send()
        label_copy1(1, other_y, y).wait_send()
        label_copy2(other_y, y).wait_send()

        @pl.loop(0, SIDE)
        def _(source):
            second_a(source, other_y, y).wait_send()
            second_b(source, other_z, z).wait_send()

    @pl.loop(1, freqs)
    def _(k):
        other = lax.rem(mine + k, freqs)
        sum_copy(other, other).wait_recv()
        sum_copy(other, mine).wait_send()

    result = gathered[0]
    for row in range(1, freqs):
        result = result + gathered[row]
    out_ref[...] = result


def on_device(
    forward_fields, adjoint_panels, residual_blocks, residual_columns, panel_brick, panel_receiver
):
    bricks, freqs = lax.axis_size("brick"), lax.axis_size("freq")
    held, span = adjoint_panels.shape[1], adjoint_panels.shape[3]
    cells = span // 3
    tx = forward_fields.shape[3]
    fields = forward_fields[0, 0].reshape(2 * tx, span)
    blocks = residual_blocks[0, 0]
    slots = bricks * SLOTS
    half = (SIDE, SIDE, SLOTS, span)
    any_space = pl.BlockSpec(memory_space=pl.ANY)
    vmem = pl.BlockSpec(memory_space=pltpu.VMEM)
    in_specs = [
        pl.BlockSpec(memory_space=pltpu.SMEM), vmem, vmem, any_space, any_space, any_space,
    ]
    loaded = [
        pltpu.VMEM((held, 2, span), jnp.bfloat16),
        pltpu.VMEM((2, held, span), jnp.bfloat16),
        pltpu.VMEM(fields.shape, jnp.bfloat16),
        pltpu.VMEM(blocks.shape, jnp.bfloat16),
    ]
    halves = [pltpu.VMEM(half, jnp.bfloat16)] * 2
    arrived = [pltpu.VMEM((bricks, SLOTS, span), jnp.bfloat16)] * 2
    work = [
        pltpu.VMEM((2, tx, 512), jnp.bfloat16),
        pltpu.VMEM((2, slots, 2 * tx), jnp.bfloat16),
        pltpu.VMEM((2, slots, span), jnp.float32),
        pltpu.VMEM((SLOTS, cells), jnp.float32),
        pltpu.VMEM((1, cells), jnp.float32),
        pltpu.VMEM((freqs, 1, cells), jnp.float32),
    ]

    def dma(*shape):
        return pltpu.SemaphoreType.DMA(shape)

    args = (
        residual_columns.transpose(2, 0, 1),
        panel_brick.reshape(1, held),
        panel_receiver.reshape(1, held),
        adjoint_panels[0],
        fields,
        blocks,
    )
    gradient = jax.ShapeDtypeStruct((1, cells), jnp.float32)
    summed, flag = pl.pallas_call(
        functools.partial(compact_kernel, freqs),
        out_shape=[gradient, jax.ShapeDtypeStruct((1, 128), jnp.int32)],
        in_specs=in_specs,
        out_specs=[vmem, vmem],
        scratch_shapes=[
            *loaded,
            pltpu.VMEM((4, CAPS[0], span), jnp.bfloat16),
            *[pltpu.VMEM((4, cap, span), jnp.bfloat16) for cap in CAPS],
            *halves,
            *arrived,
            pltpu.VMEM((2, SIDE, 128), jnp.int32),
            pltpu.VMEM((2, SIDE, 128), jnp.int32),
            pltpu.VMEM((SIDE, SIDE, 128), jnp.int32),
            *work,
            dma(3),
            *[dma(2, SIDE)] * 2,
            *[dma(SIDE)] * 2,
            *[dma(4 * STEPS * STEPS)] * 2,
            *[dma(bricks)] * 4,
            *[dma(freqs)] * 2,
        ],
        compiler_params=pltpu.CompilerParams(collective_id=0, has_side_effects=True),
        name="compact_exchange",
    )(*args)

    def padded():
        return pl.pallas_call(
            functools.partial(padded_kernel, freqs),
            out_shape=gradient,
            in_specs=in_specs,
            out_specs=vmem,
            scratch_shapes=[
                *loaded,
                *halves,
                *halves,
                *arrived,
                pltpu.VMEM((SIDE, 128), jnp.int32),
                pltpu.VMEM((SIDE, 128), jnp.int32),
                pltpu.VMEM((SIDE, SIDE, 128), jnp.int32),
                *work,
                dma(3),
                *[dma(SIDE)] * 8,
                *[dma(bricks)] * 4,
                *[dma(freqs)] * 2,
            ],
            compiler_params=pltpu.CompilerParams(collective_id=1, has_side_effects=True),
            name="padded_exchange",
        )(*args)

    summed = lax.cond(flag[0, 0] > 0, padded, lambda: summed)
    share = cells // freqs
    return lax.dynamic_slice_in_dim(summed[0], lax.axis_index("freq") * share, share, 0)


def solution(mesh):
    placed = (
        P("freq", "brick", None, None, None),
        P("freq", "brick", None, None),
        P("freq", "brick", None, None, None, None),
        P("brick", None, None),
        P("brick", None),
        P("brick"),
    )
    return jax.shard_map(
        on_device, mesh=mesh, in_specs=placed, out_specs=P(("brick", "freq")), check_vma=False
    )
```

```python
import functools

import jax
import jax.numpy as jnp
from jax import lax
from jax.experimental import pallas as pl
from jax.experimental.pallas import tpu as pltpu
from jax.sharding import PartitionSpec as P

SIDE = 8
SLOTS = 8
MESH = pl.DeviceIdType.MESH
CAPS = (128, 104, 72, 40)
EDGES = (0, 40, 72, 104, 128)
STEPS = len(CAPS)
START_LANE, SPLIT_LANE, FLAG_LANE = 64, 65, 127


def zigzag(step):
    half = (step + 1) // 2
    return 4 + half * (1 - 2 * lax.rem(step, 2))


def padded_kernel(
    freqs, columns_ref, target_ref, receiver_ref, panels_hbm, fields_hbm, blocks_hbm,
    out_ref,
    stored, panels, fields, blocks, out_a, out_b, mid_a, mid_b, in_a, in_b, labels_own, labels_mid,
    labels_in, dense, left, product, total, partial, gathered,
    load_sem, label_send1, label_recv1, label_send2, label_recv2,
    send1_a, recv1_a, send1_b, recv1_b, send2_a, recv2_a, send2_b, recv2_b,
    sum_send_sem, sum_recv_sem,
):
    me = lax.axis_index("brick")
    mine = lax.axis_index("freq")
    z, y = me // SIDE, lax.rem(me, SIDE)
    held = panels.shape[1]
    span = fields.shape[1]
    cells = span // 3
    tx = fields.shape[0] // 2

    def remote(src, dst, send, recv, **where):
        return pltpu.make_async_remote_copy(
            src_ref=src, dst_ref=dst, send_sem=send, recv_sem=recv,
            device_id=where, device_id_type=MESH,
        )

    def at(row, column):
        return row * SIDE + column

    def around(here, step):
        return lax.rem(here + zigzag(step), SIDE)

    def back(here, step):
        return lax.rem(here - zigzag(step) + SIDE, SIDE)

    loads = [
        pltpu.make_async_copy(panels_hbm, stored, load_sem.at[0]),
        pltpu.make_async_copy(blocks_hbm, blocks, load_sem.at[1]),
        pltpu.make_async_copy(fields_hbm, fields, load_sem.at[2]),
    ]
    for load in loads:
        load.start()

    barrier = pltpu.get_barrier_semaphore()

    @pl.loop(1, SIDE)
    def _(k):
        other_z, other_y = lax.rem(z + k, SIDE), lax.rem(y + k, SIDE)
        pl.semaphore_signal(
            barrier, inc=1, device_id={"brick": at(other_z, y)}, device_id_type=MESH
        )
        pl.semaphore_signal(
            barrier, inc=1, device_id={"brick": at(z, other_y)}, device_id_type=MESH
        )

    @pl.loop(1, freqs)
    def _(k):
        pl.semaphore_signal(
            barrier, inc=1, device_id={"freq": lax.rem(mine + k, freqs)}, device_id_type=MESH
        )

    target = target_ref[...]
    down = lax.broadcasted_iota(jnp.int32, (held, held), 0)
    across = lax.broadcasted_iota(jnp.int32, (held, held), 1)
    diagonal = down == across
    target_col = jnp.sum(jnp.where(diagonal, target, 0), axis=1, keepdims=True)
    same = target_col == target
    rank = jnp.sum(jnp.where(same & (down < across), 1, 0), axis=0, keepdims=True)
    rank_col = jnp.sum(jnp.where(same & (across < down), 1, 0), axis=1, keepdims=True)
    target_z, target_y = target // SIDE, lax.rem(target, SIDE)
    place_a = target * SLOTS + rank
    place_b = (target_y * SIDE + target_z) * SLOTS + rank

    value = receiver_ref[...] + 1
    names = lax.broadcasted_iota(jnp.int32, (SIDE, held), 0) == target_z
    lanes = lax.broadcasted_iota(jnp.int32, (held, 128), 1)
    by_lane = lax.rem(target_col, SIDE) * SLOTS + rank_col == lanes
    by_lane = by_lane.astype(jnp.float32).astype(jnp.bfloat16)
    high = jnp.where(names, value // 16, 0).astype(jnp.float32).astype(jnp.bfloat16)
    low = jnp.where(names, lax.rem(value, 16), 0).astype(jnp.float32).astype(jnp.bfloat16)
    high = jnp.dot(high, by_lane, preferred_element_type=jnp.float32)
    low = jnp.dot(low, by_lane, preferred_element_type=jnp.float32)
    labels_own[...] = (high * 16.0 + low).astype(jnp.int32)

    def label_copy1(other, row):
        return remote(
            labels_own.at[pl.ds(other, 1)], labels_mid.at[pl.ds(row, 1)],
            label_send1.at[other], label_recv1.at[row], brick=at(other, y),
        )

    def label_copy2(other, row):
        return remote(
            labels_mid, labels_in.at[row],
            label_send2.at[other], label_recv2.at[row], brick=at(z, other),
        )

    def first_a(other, row):
        return remote(
            out_a.at[other], mid_a.at[row], send1_a.at[other], recv1_a.at[row],
            brick=at(other, y),
        )

    def first_b(other, row):
        return remote(
            out_b.at[other], mid_b.at[row], send1_b.at[other], recv1_b.at[row],
            brick=at(z, other),
        )

    def second_a(block, source, other, column):
        index = at(column, source)
        return remote(
            block.at[other], in_a.at[index], send2_a.at[at(source, other)], recv2_a.at[index],
            brick=at(z, other),
        )

    def second_b(block, source, other, row):
        index = at(source, row)
        return remote(
            block.at[other], in_b.at[index], send2_b.at[at(source, other)], recv2_b.at[index],
            brick=at(other, y),
        )

    def build(group, place, part, into):
        slots = lax.broadcasted_iota(jnp.int32, (SIDE * SLOTS, held), 0) + group * (SIDE * SLOTS)
        select = (slots == place).astype(jnp.float32).astype(jnp.bfloat16)
        rows = jnp.dot(
            select, panels[part], preferred_element_type=jnp.float32,
        )
        into[group] = rows.reshape(SIDE, SLOTS, span).astype(jnp.bfloat16)

    loads[0].wait()
    panels[...] = jnp.swapaxes(stored[...], 0, 1)
    build(around(z, 0), place_a, 0, out_a)
    build(around(y, 0), place_b, 1, out_b)
    pl.semaphore_wait(barrier, 2 * (SIDE - 1) + freqs - 1)

    @pl.loop(1, SIDE)
    def _(k):
        label_copy1(lax.rem(z + k, SIDE), z).start()

    @pl.loop(0, SIDE)
    def _(step):
        other_z, other_y = around(z, step), around(y, step)

        @pl.when(step > 0)
        def _():
            build(other_z, place_a, 0, out_a)
            build(other_y, place_b, 1, out_b)

        @pl.when(step < SIDE - 1)
        def _():
            first_a(other_z, z).start()
            first_b(other_y, y).start()

    @pl.loop(0, SIDE - 1)
    def _(step):
        second_a(out_a.at[z], z, around(y, step), y).start()
        second_b(out_b.at[y], y, around(z, step), z).start()

    labels_mid[pl.ds(z, 1)] = labels_own[pl.ds(z, 1)]

    @pl.loop(1, SIDE)
    def _(k):
        other = lax.rem(z + k, SIDE)
        label_copy1(other, other).wait_recv()

    @pl.loop(1, SIDE)
    def _(k):
        label_copy2(lax.rem(y + k, SIDE), y).start()

    labels_in[y] = labels_mid[...]

    loads[1].wait()
    for k in range(columns_ref.shape[2]):
        for r in range(SIDE):
            tile = jnp.zeros((blocks.shape[2], blocks.shape[3]), jnp.bfloat16)
            for j in range(columns_ref.shape[0]):
                tile = jnp.where(columns_ref[j, 0, k] == r, blocks[k, j], tile)
            dense[0, pl.ds(k * 64, 64), pl.ds(r * 64, 64)] = tile[:, :64]
            dense[1, pl.ds(k * 64, 64), pl.ds(r * 64, 64)] = tile[:, 64:]

    @pl.loop(1, SIDE)
    def _(k):
        other = lax.rem(y + k, SIDE)
        label_copy2(other, other).wait_recv()

    slots = SIDE * SIDE * SLOTS
    named = labels_in[...].reshape(SIDE * SIDE, 128)
    pick = lax.broadcasted_iota(jnp.int32, (SIDE * SIDE, SLOTS, 128), 1) + y * SLOTS
    pick = pick == lax.broadcasted_iota(jnp.int32, (SIDE * SIDE, SLOTS, 128), 2)
    label = jnp.sum(jnp.where(pick, named[:, None, :], 0), axis=2, keepdims=True)
    label = label.reshape(slots, 1) - 1
    receivers = lax.broadcasted_iota(jnp.int32, (slots, dense.shape[2]), 1)
    onehot = (receivers == label).astype(jnp.float32).astype(jnp.bfloat16)
    dims = (((1,), (1,)), ((), ()))
    real = lax.dot_general(onehot, dense[0], dims, preferred_element_type=jnp.float32)
    imag = lax.dot_general(onehot, dense[1], dims, preferred_element_type=jnp.float32)
    left[0, :, pl.ds(0, tx)] = real.astype(jnp.bfloat16)
    left[0, :, pl.ds(tx, tx)] = (-imag).astype(jnp.bfloat16)
    left[1, :, pl.ds(0, tx)] = imag.astype(jnp.bfloat16)
    left[1, :, pl.ds(tx, tx)] = real.astype(jnp.bfloat16)

    loads[2].wait()

    def multiply(piece):
        part, tile = piece // 4, lax.rem(piece, 4)
        rows = pl.ds(pl.multiple_of(tile * 128, 128), 128)
        product[part, rows] = jnp.dot(
            left[part, rows], fields[...], preferred_element_type=jnp.float32
        )

    def term(part, block, index):
        rows = pl.ds(pl.multiple_of(index * SLOTS, SLOTS), SLOTS)
        both = product[part, rows] * block.astype(jnp.float32)
        return both[:, :cells] + both[:, cells : 2 * cells] + both[:, 2 * cells :]

    @pl.loop(0, SIDE - 1)
    def _(step):
        source_z, source_y = back(z, step), back(y, step)
        first_a(source_z, source_z).wait_recv()

        @pl.loop(0, SIDE - 1)
        def _(inner):
            second_a(mid_a.at[source_z], source_z, around(y, inner), y).start()

        first_b(source_y, source_y).wait_recv()

        @pl.loop(0, SIDE - 1)
        def _(inner):
            second_b(mid_b.at[source_y], source_y, around(z, inner), z).start()

        multiply(step)

    multiply(SIDE - 1)
    total[...] = term(0, out_a[z, y], at(y, z)) - term(1, out_b[y, z], at(y, z))

    @pl.loop(0, SIDE - 1)
    def _(step):
        source_z, source_y = back(z, step), back(y, step)
        total[...] += term(0, mid_a[source_z, y], at(y, source_z)) - term(
            1, mid_b[source_y, z], at(source_y, z)
        )

    @pl.loop(0, SIDE)
    def _(step):
        source = lax.rem(step + SIDE - 1, SIDE)
        source_z, source_y = back(z, source), back(y, source)

        @pl.loop(0, SIDE - 1)
        def _(inner):
            column, row = back(y, inner), back(z, inner)
            index_a, index_b = at(column, source_z), at(source_y, row)
            second_a(mid_a.at[source_z], source_z, column, column).wait_recv()
            second_b(mid_b.at[source_y], source_y, row, row).wait_recv()
            total[...] += term(0, in_a[index_a], index_a) - term(1, in_b[index_b], index_b)

    partial[...] = jnp.sum(total[...], axis=0, keepdims=True)

    def sum_copy(other, row):
        return remote(
            partial, gathered.at[row], sum_send_sem.at[other], sum_recv_sem.at[row], freq=other
        )

    @pl.loop(1, freqs)
    def _(k):
        sum_copy(lax.rem(mine + k, freqs), mine).start()

    gathered[mine] = partial[...]

    @pl.loop(1, SIDE)
    def _(k):
        other_z, other_y = lax.rem(z + k, SIDE), lax.rem(y + k, SIDE)
        label_copy1(other_z, z).wait_send()
        label_copy2(other_y, y).wait_send()
        first_a(other_z, z).wait_send()
        first_b(other_y, y).wait_send()

        @pl.loop(0, SIDE)
        def _(source):
            second_a(mid_a.at[source], source, other_y, y).wait_send()
            second_b(mid_b.at[source], source, other_z, z).wait_send()

    @pl.loop(1, freqs)
    def _(k):
        other = lax.rem(mine + k, freqs)
        sum_copy(other, other).wait_recv()
        sum_copy(other, mine).wait_send()

    result = gathered[0]
    for row in range(1, freqs):
        result = result + gathered[row]
    out_ref[...] = result


def count(mask, axis):
    return jnp.sum(jnp.where(mask, 1, 0), axis=axis, keepdims=True)


def iota(shape, axis):
    return lax.broadcasted_iota(jnp.int32, shape, axis)


def onehot(mask):
    return mask.astype(jnp.float32).astype(jnp.bfloat16)


def make_lists(axis_row, axis_col, slot_row, slot_col, here):
    off_row = lax.rem(axis_row - here + SIDE, SIDE)
    off_col = lax.rem(axis_col - here + SIDE, SIDE)
    half = SIDE // 2
    far_row, far_col = off_row == half, off_col == half
    index_row = count(far_col & (slot_col < slot_row), 0)
    index_col = count(far_row & (slot_row < slot_col), 1)
    number = count(far_row, 1)
    up = count((off_row >= 1) & (off_row < half), 1)
    down = count(off_row > half, 1)
    split = jnp.minimum(jnp.maximum(down + number - up, 0) // 2, number)

    def which(off, index):
        plus = ((off >= 1) & (off < half)) | ((off == half) & (index < split))
        minus = (off > half) | ((off == half) & (index >= split))
        return jnp.where(plus, 0, jnp.where(minus, 1, 2))

    list_row, list_col = which(off_row, index_row), which(off_col, index_col)
    dist_row = jnp.minimum(off_row, SIDE - off_row)
    dist_col = jnp.minimum(off_col, SIDE - off_col)
    key_row = (half - dist_row) * (SIDE * SLOTS) + slot_row
    key_col = (half - dist_col) * (SIDE * SLOTS) + slot_col
    place = count((list_col == list_row) & (key_col < key_row), 0)

    over = jnp.zeros((1, 1), jnp.int32)
    for one in range(2):
        for step in range(STEPS):
            length = count((list_row == one) & (dist_row > step), 1)
            over = jnp.maximum(over, jnp.where(length > CAPS[step], 1, 0))

    row = lax.rem(iota((SIDE, 1), 0) - here + SIDE, SIDE)
    row_list = jnp.where(row < half, 0, 1)
    row_dist = jnp.minimum(row, SIDE - row)
    start = count((list_row == row_list) & (dist_row > row_dist), 1)
    return list_row, place, start, split, over


def compact_kernel(
    freqs, columns_ref, target_ref, receiver_ref, panels_hbm, fields_hbm, blocks_hbm,
    out_ref, flag_ref,
    stored, panels, fields, blocks, lists, ring1, ring2, ring3, ring4, mid_a, mid_b, in_a, in_b,
    labels_own, labels_mid, labels_in, dense, left, product, total, partial, gathered,
    load_sem, label_send1, label_recv1, label_send2, label_recv2, hop_send, hop_recv,
    send2_a, recv2_a, send2_b, recv2_b, sum_send_sem, sum_recv_sem,
):
    me = lax.axis_index("brick")
    mine = lax.axis_index("freq")
    z, y = me // SIDE, lax.rem(me, SIDE)
    here = (z, y)
    rings = (ring1, ring2, ring3, ring4)
    mids = (mid_a, mid_b)
    held = panels.shape[1]
    span = fields.shape[1]
    cells = span // 3
    tx = fields.shape[0] // 2
    group = SIDE * SLOTS

    def remote(src, dst, send, recv, **where):
        return pltpu.make_async_remote_copy(
            src_ref=src, dst_ref=dst, send_sem=send, recv_sem=recv,
            device_id=where, device_id_type=MESH,
        )

    def at(row, column):
        return row * SIDE + column

    def along(path, other):
        return at(other, y) if path == 0 else at(z, other)

    def around(start, step):
        return lax.rem(start + zigzag(step), SIDE)

    def back(start, step):
        return lax.rem(start - zigzag(step) + SIDE, SIDE)

    loads = [
        pltpu.make_async_copy(panels_hbm, stored, load_sem.at[0]),
        pltpu.make_async_copy(blocks_hbm, blocks, load_sem.at[1]),
        pltpu.make_async_copy(fields_hbm, fields, load_sem.at[2]),
    ]
    for load in loads:
        load.start()

    barrier = pltpu.get_barrier_semaphore()

    @pl.loop(1, SIDE)
    def _(k):
        for path in range(2):
            other = lax.rem(here[path] + k, SIDE)
            pl.semaphore_signal(
                barrier, inc=1, device_id={"brick": along(path, other)}, device_id_type=MESH
            )

    @pl.loop(1, freqs)
    def _(k):
        pl.semaphore_signal(
            barrier, inc=1, device_id={"freq": lax.rem(mine + k, freqs)}, device_id_type=MESH
        )

    target = target_ref[...]
    down, across = iota((held, held), 0), iota((held, held), 1)
    target_col = jnp.sum(jnp.where(down == across, target, 0), axis=1, keepdims=True)
    same = target_col == target
    rank, rank_col = count(same & (down < across), 0), count(same & (across < down), 1)
    axis_row = (target // SIDE, lax.rem(target, SIDE))
    axis_col = (target_col // SIDE, lax.rem(target_col, SIDE))
    slot_row = tuple(axis_row[1 - path] * SLOTS + rank for path in range(2))
    slot_col = tuple(axis_col[1 - path] * SLOTS + rank_col for path in range(2))

    loads[0].wait()
    panels[...] = jnp.swapaxes(stored[...], 0, 1)
    value = receiver_ref[...] + 1
    over = jnp.zeros((1, 1), jnp.int32)
    lanes = iota((SIDE, 128), 1)
    rows = []
    for path in range(2):
        list_row, place, start, split, too_long = make_lists(
            axis_row[path], axis_col[path], slot_row[path], slot_col[path], here[path]
        )
        over = jnp.maximum(over, too_long)
        for one in range(2):
            select = onehot((iota((CAPS[0], held), 0) == place) & (list_row == one))
            found = jnp.dot(select, panels[path], preferred_element_type=jnp.float32)
            found = found.reshape(CAPS[0] // SLOTS, SLOTS, span)
            lists[2 * path + one] = found.astype(jnp.bfloat16)
        names = iota((SIDE, held), 0) == axis_row[path]
        by_lane = onehot(slot_col[path] == iota((held, 128), 1))
        high = jnp.where(names, value // 16, 0).astype(jnp.float32).astype(jnp.bfloat16)
        low = jnp.where(names, lax.rem(value, 16), 0).astype(jnp.float32).astype(jnp.bfloat16)
        high = jnp.dot(high, by_lane, preferred_element_type=jnp.float32)
        low = jnp.dot(low, by_lane, preferred_element_type=jnp.float32)
        named = (high * 16.0 + low).astype(jnp.int32)
        named = jnp.where(lanes == START_LANE, start, named)
        rows.append(jnp.where(lanes == SPLIT_LANE, split, named))
    labels_own[0] = jnp.where(lanes == FLAG_LANE, over, rows[0])
    labels_own[1] = rows[1]

    def label_copy1(path, other, row):
        return remote(
            labels_own.at[path, pl.ds(other, 1)], labels_mid.at[path, pl.ds(row, 1)],
            label_send1.at[path, other], label_recv1.at[path, row],
            brick=along(path, other),
        )

    def label_copy2(other, row):
        return remote(
            labels_mid.at[0], labels_in.at[row],
            label_send2.at[other], label_recv2.at[row], brick=at(z, other),
        )

    def hop(path, one, step, chunk):
        part = 2 * path + one
        piece = pl.ds(EDGES[chunk] // SLOTS, (EDGES[chunk + 1] - EDGES[chunk]) // SLOTS)
        source = lists if step == 0 else rings[step - 1]
        index = (part * STEPS + step) * STEPS + chunk
        other = lax.rem(here[path] + (1 if one == 0 else SIDE - 1), SIDE)
        return remote(
            source.at[part, piece], rings[step].at[part, piece],
            hop_send.at[index], hop_recv.at[index], brick=along(path, other),
        )

    ways = [(path, one) for path in range(2) for one in range(2)]

    def second_a(source, other, column):
        index = at(column, source)
        return remote(
            mid_a.at[source, other], in_a.at[index],
            send2_a.at[at(source, other)], recv2_a.at[index], brick=at(z, other),
        )

    def second_b(source, other, row):
        index = at(source, row)
        return remote(
            mid_b.at[source, other], in_b.at[index],
            send2_b.at[at(source, other)], recv2_b.at[index], brick=at(other, y),
        )

    def pass_on(path, source):
        @pl.loop(0, SIDE - 1)
        def _(inner):
            if path == 0:
                second_a(source, around(y, inner), y).start()
            else:
                second_b(source, around(z, inner), z).start()

    def spread(path, step, one):
        source = lax.rem(here[path] + (SIDE - step - 1 if one == 0 else step + 1), SIDE)
        row = labels_mid[path, pl.ds(source, 1)]
        lane, slot = iota((group, 128), 1), iota((group, 128), 0)
        filled = row > 0
        full = count((lane == slot) & filled, 1) > 0
        index = count((lane < slot) & filled, 1)
        single = iota((1, 128), 1)
        if step < STEPS - 1:
            index = index + jnp.sum(jnp.where(single == START_LANE, row, 0), axis=1, keepdims=True)
        else:
            split = jnp.sum(jnp.where(single == SPLIT_LANE, row, 0), axis=1, keepdims=True)
            if one == 0:
                full = full & (index < split)
            else:
                full = full & (index >= split)
                index = index - split
        select = onehot((iota((group, CAPS[step]), 1) == index) & full)
        rows = rings[step][2 * path + one].astype(jnp.float32).reshape(CAPS[step], span)
        return source, jnp.dot(
            select, rows.astype(jnp.bfloat16), preferred_element_type=jnp.float32
        )

    def put(path, source, found):
        mids[path][source] = found.reshape(SIDE, SLOTS, span).astype(jnp.bfloat16)

    def deliver(step):
        for path in range(2):
            if step < STEPS - 1:
                for one in range(2):
                    source, found = spread(path, step, one)
                    put(path, source, found)
                    pass_on(path, source)
            else:
                source, found = spread(path, step, 0)
                put(path, source, found + spread(path, step, 1)[1])
                pass_on(path, source)

    def receive(step):
        for chunk in range(STEPS - step):
            for path, one in ways:
                hop(path, one, step, chunk).wait_recv()
                if chunk < STEPS - step - 1:
                    hop(path, one, step + 1, chunk).start()

    pl.semaphore_wait(barrier, 2 * (SIDE - 1) + freqs - 1)

    @pl.loop(1, SIDE)
    def _(k):
        for path in range(2):
            label_copy1(path, lax.rem(here[path] + k, SIDE), here[path]).start()

    for chunk in range(STEPS):
        for path, one in ways:
            hop(path, one, 0, chunk).start()

    for path in range(2):
        select = onehot((iota((group, held), 0) == slot_row[path]) & (axis_row[path] == here[path]))
        put(path, here[path], jnp.dot(select, panels[path], preferred_element_type=jnp.float32))
        labels_mid[path, pl.ds(here[path], 1)] = labels_own[path, pl.ds(here[path], 1)]

    @pl.loop(1, SIDE)
    def _(k):
        for path in range(2):
            other = lax.rem(here[path] + k, SIDE)
            label_copy1(path, other, other).wait_recv()

    @pl.loop(1, SIDE)
    def _(k):
        label_copy2(lax.rem(y + k, SIDE), y).start()

    labels_in[y] = labels_mid[0]

    receive(0)
    for path in range(2):
        pass_on(path, here[path])
    deliver(0)

    loads[1].wait()
    for k in range(columns_ref.shape[2]):
        for r in range(SIDE):
            tile = jnp.zeros((blocks.shape[2], blocks.shape[3]), jnp.bfloat16)
            for j in range(columns_ref.shape[0]):
                tile = jnp.where(columns_ref[j, 0, k] == r, blocks[k, j], tile)
            dense[0, pl.ds(k * 64, 64), pl.ds(r * 64, 64)] = tile[:, :64]
            dense[1, pl.ds(k * 64, 64), pl.ds(r * 64, 64)] = tile[:, 64:]

    receive(1)
    deliver(1)

    @pl.loop(1, SIDE)
    def _(k):
        other = lax.rem(y + k, SIDE)
        label_copy2(other, other).wait_recv()

    slots = SIDE * group
    named = labels_in[...].reshape(SIDE * SIDE, 128)
    flags = jnp.where(iota((SIDE * SIDE, 128), 1) == FLAG_LANE, named, 0)
    flag = jnp.max(jnp.max(flags, axis=1, keepdims=True), axis=0, keepdims=True)
    flag_ref[...] = jnp.broadcast_to(flag, flag_ref.shape)
    pick = iota((SIDE * SIDE, SLOTS, 128), 1) + y * SLOTS == iota((SIDE * SIDE, SLOTS, 128), 2)
    label = jnp.sum(jnp.where(pick, named[:, None, :], 0), axis=2, keepdims=True)
    label = label.reshape(slots, 1) - 1
    chosen = onehot(iota((slots, dense.shape[2]), 1) == label)
    dims = (((1,), (1,)), ((), ()))
    real = lax.dot_general(chosen, dense[0], dims, preferred_element_type=jnp.float32)
    imag = lax.dot_general(chosen, dense[1], dims, preferred_element_type=jnp.float32)
    left[0, :, pl.ds(0, tx)] = real.astype(jnp.bfloat16)
    left[0, :, pl.ds(tx, tx)] = (-imag).astype(jnp.bfloat16)
    left[1, :, pl.ds(0, tx)] = imag.astype(jnp.bfloat16)
    left[1, :, pl.ds(tx, tx)] = real.astype(jnp.bfloat16)

    receive(2)
    deliver(2)
    receive(3)
    deliver(3)

    loads[2].wait()

    @pl.loop(0, SIDE)
    def _(piece):
        part, tile = piece // 4, lax.rem(piece, 4)
        rows = pl.ds(pl.multiple_of(tile * 128, 128), 128)
        product[part, rows] = jnp.dot(
            left[part, rows], fields[...], preferred_element_type=jnp.float32
        )

    def term(part, block, index):
        rows = pl.ds(pl.multiple_of(index * SLOTS, SLOTS), SLOTS)
        both = product[part, rows] * block.astype(jnp.float32)
        return both[:, :cells] + both[:, cells : 2 * cells] + both[:, 2 * cells :]

    total[...] = jnp.zeros_like(total)

    @pl.loop(0, SIDE)
    def _(source):
        total[...] += term(0, mid_a[source, y], at(y, source)) - term(
            1, mid_b[source, z], at(source, z)
        )

    @pl.loop(0, SIDE)
    def _(step):
        source_z, source_y = back(z, SIDE - 1 - step), back(y, SIDE - 1 - step)

        @pl.loop(0, SIDE - 1)
        def _(inner):
            column, row = back(y, inner), back(z, inner)
            index_a, index_b = at(column, source_z), at(source_y, row)
            second_a(source_z, column, column).wait_recv()
            second_b(source_y, row, row).wait_recv()
            total[...] += term(0, in_a[index_a], index_a) - term(1, in_b[index_b], index_b)

    partial[...] = jnp.sum(total[...], axis=0, keepdims=True)

    def sum_copy(other, row):
        return remote(
            partial, gathered.at[row], sum_send_sem.at[other], sum_recv_sem.at[row], freq=other
        )

    @pl.loop(1, freqs)
    def _(k):
        sum_copy(lax.rem(mine + k, freqs), mine).start()

    gathered[mine] = partial[...]

    for step in range(STEPS):
        for chunk in range(STEPS - step):
            for path, one in ways:
                hop(path, one, step, chunk).wait_send()

    @pl.loop(1, SIDE)
    def _(k):
        other_z, other_y = lax.rem(z + k, SIDE), lax.rem(y + k, SIDE)
        label_copy1(0, other_z, z).wait_send()
        label_copy1(1, other_y, y).wait_send()
        label_copy2(other_y, y).wait_send()

        @pl.loop(0, SIDE)
        def _(source):
            second_a(source, other_y, y).wait_send()
            second_b(source, other_z, z).wait_send()

    @pl.loop(1, freqs)
    def _(k):
        other = lax.rem(mine + k, freqs)
        sum_copy(other, other).wait_recv()
        sum_copy(other, mine).wait_send()

    result = gathered[0]
    for row in range(1, freqs):
        result = result + gathered[row]
    out_ref[...] = result


def on_device(
    forward_fields, adjoint_panels, residual_blocks, residual_columns, panel_brick, panel_receiver
):
    bricks, freqs = lax.axis_size("brick"), lax.axis_size("freq")
    held, span = adjoint_panels.shape[1], adjoint_panels.shape[3]
    cells = span // 3
    tx = forward_fields.shape[3]
    fields = forward_fields[0, 0].reshape(2 * tx, span)
    blocks = residual_blocks[0, 0]
    slots = bricks * SLOTS
    half = (SIDE, SIDE, SLOTS, span)
    any_space = pl.BlockSpec(memory_space=pl.ANY)
    vmem = pl.BlockSpec(memory_space=pltpu.VMEM)
    in_specs = [
        pl.BlockSpec(memory_space=pltpu.SMEM), vmem, vmem, any_space, any_space, any_space,
    ]
    loaded = [
        pltpu.VMEM((held, 2, span), jnp.bfloat16),
        pltpu.VMEM((2, held, span), jnp.bfloat16),
        pltpu.VMEM(fields.shape, jnp.bfloat16),
        pltpu.VMEM(blocks.shape, jnp.bfloat16),
    ]
    halves = [pltpu.VMEM(half, jnp.bfloat16)] * 2
    arrived = [pltpu.VMEM((bricks, SLOTS, span), jnp.bfloat16)] * 2
    work = [
        pltpu.VMEM((2, tx, 512), jnp.bfloat16),
        pltpu.VMEM((2, slots, 2 * tx), jnp.bfloat16),
        pltpu.VMEM((2, slots, span), jnp.float32),
        pltpu.VMEM((SLOTS, cells), jnp.float32),
        pltpu.VMEM((1, cells), jnp.float32),
        pltpu.VMEM((freqs, 1, cells), jnp.float32),
    ]

    def dma(*shape):
        return pltpu.SemaphoreType.DMA(shape)

    args = (
        residual_columns.transpose(2, 0, 1),
        panel_brick.reshape(1, held),
        panel_receiver.reshape(1, held),
        adjoint_panels[0],
        fields,
        blocks,
    )
    gradient = jax.ShapeDtypeStruct((1, cells), jnp.float32)
    summed, flag = pl.pallas_call(
        functools.partial(compact_kernel, freqs),
        out_shape=[gradient, jax.ShapeDtypeStruct((1, 128), jnp.int32)],
        in_specs=in_specs,
        out_specs=[vmem, vmem],
        scratch_shapes=[
            *loaded,
            pltpu.VMEM((4, CAPS[0] // SLOTS, SLOTS, span), jnp.bfloat16),
            *[pltpu.VMEM((4, cap // SLOTS, SLOTS, span), jnp.bfloat16) for cap in CAPS],
            *halves,
            *arrived,
            pltpu.VMEM((2, SIDE, 128), jnp.int32),
            pltpu.VMEM((2, SIDE, 128), jnp.int32),
            pltpu.VMEM((SIDE, SIDE, 128), jnp.int32),
            *work,
            dma(3),
            *[dma(2, SIDE)] * 2,
            *[dma(SIDE)] * 2,
            *[dma(4 * STEPS * STEPS)] * 2,
            *[dma(bricks)] * 4,
            *[dma(freqs)] * 2,
        ],
        compiler_params=pltpu.CompilerParams(collective_id=0, has_side_effects=True),
        name="compact_exchange",
    )(*args)

    def padded():
        return pl.pallas_call(
            functools.partial(padded_kernel, freqs),
            out_shape=gradient,
            in_specs=in_specs,
            out_specs=vmem,
            scratch_shapes=[
                *loaded,
                *halves,
                *halves,
                *arrived,
                pltpu.VMEM((SIDE, 128), jnp.int32),
                pltpu.VMEM((SIDE, 128), jnp.int32),
                pltpu.VMEM((SIDE, SIDE, 128), jnp.int32),
                *work,
                dma(3),
                *[dma(SIDE)] * 8,
                *[dma(bricks)] * 4,
                *[dma(freqs)] * 2,
            ],
            compiler_params=pltpu.CompilerParams(collective_id=1, has_side_effects=True),
            name="padded_exchange",
        )(*args)

    summed = lax.cond(flag[0, 0] > 0, padded, lambda: summed)
    share = cells // freqs
    return lax.dynamic_slice_in_dim(summed[0], lax.axis_index("freq") * share, share, 0)


def solution(mesh):
    placed = (
        P("freq", "brick", None, None, None),
        P("freq", "brick", None, None),
        P("freq", "brick", None, None, None, None),
        P("brick", None, None),
        P("brick", None),
        P("brick"),
    )
    return jax.shard_map(
        on_device, mesh=mesh, in_specs=placed, out_specs=P(("brick", "freq")), check_vma=False
    )
```

```python
import functools

import jax
import jax.numpy as jnp
from jax import lax
from jax.experimental import pallas as pl
from jax.experimental.pallas import tpu as pltpu
from jax.sharding import PartitionSpec as P

SIDE = 8
SLOTS = 8
MESH = pl.DeviceIdType.MESH
CAPS = (128, 104, 72, 40)
EDGES = (0, 40, 72, 104, 128)
STEPS = len(CAPS)
START_LANE, SPLIT_LANE, FLAG_LANE = 64, 65, 127


def zigzag(step):
    half = (step + 1) // 2
    return 4 + half * (1 - 2 * lax.rem(step, 2))


def padded_kernel(
    freqs, columns_ref, target_ref, receiver_ref, panels_hbm, fields_hbm, blocks_hbm,
    out_ref,
    stored, panels, fields, blocks, out_a, out_b, mid_a, mid_b, in_a, in_b, labels_own, labels_mid,
    labels_in, dense, left, product, total, partial, gathered,
    load_sem, label_send1, label_recv1, label_send2, label_recv2,
    send1_a, recv1_a, send1_b, recv1_b, send2_a, recv2_a, send2_b, recv2_b,
    sum_send_sem, sum_recv_sem,
):
    me = lax.axis_index("brick")
    mine = lax.axis_index("freq")
    z, y = me // SIDE, lax.rem(me, SIDE)
    held = panels.shape[1]
    span = fields.shape[1]
    cells = span // 3
    tx = fields.shape[0] // 2

    def remote(src, dst, send, recv, **where):
        return pltpu.make_async_remote_copy(
            src_ref=src, dst_ref=dst, send_sem=send, recv_sem=recv,
            device_id=where, device_id_type=MESH,
        )

    def at(row, column):
        return row * SIDE + column

    def around(here, step):
        return lax.rem(here + zigzag(step), SIDE)

    def back(here, step):
        return lax.rem(here - zigzag(step) + SIDE, SIDE)

    loads = [
        pltpu.make_async_copy(panels_hbm, stored, load_sem.at[0]),
        pltpu.make_async_copy(blocks_hbm, blocks, load_sem.at[1]),
        pltpu.make_async_copy(fields_hbm, fields, load_sem.at[2]),
    ]
    for load in loads:
        load.start()

    barrier = pltpu.get_barrier_semaphore()

    @pl.loop(1, SIDE)
    def _(k):
        other_z, other_y = lax.rem(z + k, SIDE), lax.rem(y + k, SIDE)
        pl.semaphore_signal(
            barrier, inc=1, device_id={"brick": at(other_z, y)}, device_id_type=MESH
        )
        pl.semaphore_signal(
            barrier, inc=1, device_id={"brick": at(z, other_y)}, device_id_type=MESH
        )

    @pl.loop(1, freqs)
    def _(k):
        pl.semaphore_signal(
            barrier, inc=1, device_id={"freq": lax.rem(mine + k, freqs)}, device_id_type=MESH
        )

    target = target_ref[...]
    down = lax.broadcasted_iota(jnp.int32, (held, held), 0)
    across = lax.broadcasted_iota(jnp.int32, (held, held), 1)
    diagonal = down == across
    target_col = jnp.sum(jnp.where(diagonal, target, 0), axis=1, keepdims=True)
    same = target_col == target
    rank = jnp.sum(jnp.where(same & (down < across), 1, 0), axis=0, keepdims=True)
    rank_col = jnp.sum(jnp.where(same & (across < down), 1, 0), axis=1, keepdims=True)
    target_z, target_y = target // SIDE, lax.rem(target, SIDE)
    place_a = target * SLOTS + rank
    place_b = (target_y * SIDE + target_z) * SLOTS + rank

    value = receiver_ref[...] + 1
    names = lax.broadcasted_iota(jnp.int32, (SIDE, held), 0) == target_z
    lanes = lax.broadcasted_iota(jnp.int32, (held, 128), 1)
    by_lane = lax.rem(target_col, SIDE) * SLOTS + rank_col == lanes
    by_lane = by_lane.astype(jnp.float32).astype(jnp.bfloat16)
    high = jnp.where(names, value // 16, 0).astype(jnp.float32).astype(jnp.bfloat16)
    low = jnp.where(names, lax.rem(value, 16), 0).astype(jnp.float32).astype(jnp.bfloat16)
    high = jnp.dot(high, by_lane, preferred_element_type=jnp.float32)
    low = jnp.dot(low, by_lane, preferred_element_type=jnp.float32)
    labels_own[...] = (high * 16.0 + low).astype(jnp.int32)

    def label_copy1(other, row):
        return remote(
            labels_own.at[pl.ds(other, 1)], labels_mid.at[pl.ds(row, 1)],
            label_send1.at[other], label_recv1.at[row], brick=at(other, y),
        )

    def label_copy2(other, row):
        return remote(
            labels_mid, labels_in.at[row],
            label_send2.at[other], label_recv2.at[row], brick=at(z, other),
        )

    def first_a(other, row):
        return remote(
            out_a.at[other], mid_a.at[row], send1_a.at[other], recv1_a.at[row],
            brick=at(other, y),
        )

    def first_b(other, row):
        return remote(
            out_b.at[other], mid_b.at[row], send1_b.at[other], recv1_b.at[row],
            brick=at(z, other),
        )

    def second_a(block, source, other, column):
        index = at(column, source)
        return remote(
            block.at[other], in_a.at[index], send2_a.at[at(source, other)], recv2_a.at[index],
            brick=at(z, other),
        )

    def second_b(block, source, other, row):
        index = at(source, row)
        return remote(
            block.at[other], in_b.at[index], send2_b.at[at(source, other)], recv2_b.at[index],
            brick=at(other, y),
        )

    def build(group, place, part, into):
        slots = lax.broadcasted_iota(jnp.int32, (SIDE * SLOTS, held), 0) + group * (SIDE * SLOTS)
        select = (slots == place).astype(jnp.float32).astype(jnp.bfloat16)
        rows = jnp.dot(
            select, panels[part], preferred_element_type=jnp.float32,
        )
        into[group] = rows.reshape(SIDE, SLOTS, span).astype(jnp.bfloat16)

    loads[0].wait()
    panels[...] = jnp.swapaxes(stored[...], 0, 1)
    build(around(z, 0), place_a, 0, out_a)
    build(around(y, 0), place_b, 1, out_b)
    pl.semaphore_wait(barrier, 2 * (SIDE - 1) + freqs - 1)

    @pl.loop(1, SIDE)
    def _(k):
        label_copy1(lax.rem(z + k, SIDE), z).start()

    @pl.loop(0, SIDE)
    def _(step):
        other_z, other_y = around(z, step), around(y, step)

        @pl.when(step > 0)
        def _():
            build(other_z, place_a, 0, out_a)
            build(other_y, place_b, 1, out_b)

        @pl.when(step < SIDE - 1)
        def _():
            first_a(other_z, z).start()
            first_b(other_y, y).start()

    @pl.loop(0, SIDE - 1)
    def _(step):
        second_a(out_a.at[z], z, around(y, step), y).start()
        second_b(out_b.at[y], y, around(z, step), z).start()

    labels_mid[pl.ds(z, 1)] = labels_own[pl.ds(z, 1)]

    @pl.loop(1, SIDE)
    def _(k):
        other = lax.rem(z + k, SIDE)
        label_copy1(other, other).wait_recv()

    @pl.loop(1, SIDE)
    def _(k):
        label_copy2(lax.rem(y + k, SIDE), y).start()

    labels_in[y] = labels_mid[...]

    loads[1].wait()
    for k in range(columns_ref.shape[2]):
        for r in range(SIDE):
            tile = jnp.zeros((blocks.shape[2], blocks.shape[3]), jnp.bfloat16)
            for j in range(columns_ref.shape[0]):
                tile = jnp.where(columns_ref[j, 0, k] == r, blocks[k, j], tile)
            dense[0, pl.ds(k * 64, 64), pl.ds(r * 64, 64)] = tile[:, :64]
            dense[1, pl.ds(k * 64, 64), pl.ds(r * 64, 64)] = tile[:, 64:]

    @pl.loop(1, SIDE)
    def _(k):
        other = lax.rem(y + k, SIDE)
        label_copy2(other, other).wait_recv()

    slots = SIDE * SIDE * SLOTS
    named = labels_in[...].reshape(SIDE * SIDE, 128)
    pick = lax.broadcasted_iota(jnp.int32, (SIDE * SIDE, SLOTS, 128), 1) + y * SLOTS
    pick = pick == lax.broadcasted_iota(jnp.int32, (SIDE * SIDE, SLOTS, 128), 2)
    label = jnp.sum(jnp.where(pick, named[:, None, :], 0), axis=2, keepdims=True)
    label = label.reshape(slots, 1) - 1
    receivers = lax.broadcasted_iota(jnp.int32, (slots, dense.shape[2]), 1)
    onehot = (receivers == label).astype(jnp.float32).astype(jnp.bfloat16)
    dims = (((1,), (1,)), ((), ()))
    real = lax.dot_general(onehot, dense[0], dims, preferred_element_type=jnp.float32)
    imag = lax.dot_general(onehot, dense[1], dims, preferred_element_type=jnp.float32)
    left[0, :, pl.ds(0, tx)] = real.astype(jnp.bfloat16)
    left[0, :, pl.ds(tx, tx)] = (-imag).astype(jnp.bfloat16)
    left[1, :, pl.ds(0, tx)] = imag.astype(jnp.bfloat16)
    left[1, :, pl.ds(tx, tx)] = real.astype(jnp.bfloat16)

    loads[2].wait()

    def multiply(piece):
        part, tile = piece // 4, lax.rem(piece, 4)
        rows = pl.ds(pl.multiple_of(tile * 128, 128), 128)
        product[part, rows] = jnp.dot(
            left[part, rows], fields[...], preferred_element_type=jnp.float32
        )

    def term(part, block, index):
        rows = pl.ds(pl.multiple_of(index * SLOTS, SLOTS), SLOTS)
        both = product[part, rows] * block.astype(jnp.float32)
        return both[:, :cells] + both[:, cells : 2 * cells] + both[:, 2 * cells :]

    @pl.loop(0, SIDE - 1)
    def _(step):
        source_z, source_y = back(z, step), back(y, step)
        first_a(source_z, source_z).wait_recv()

        @pl.loop(0, SIDE - 1)
        def _(inner):
            second_a(mid_a.at[source_z], source_z, around(y, inner), y).start()

        first_b(source_y, source_y).wait_recv()

        @pl.loop(0, SIDE - 1)
        def _(inner):
            second_b(mid_b.at[source_y], source_y, around(z, inner), z).start()

        multiply(step)

    multiply(SIDE - 1)
    total[...] = term(0, out_a[z, y], at(y, z)) - term(1, out_b[y, z], at(y, z))

    @pl.loop(0, SIDE - 1)
    def _(step):
        source_z, source_y = back(z, step), back(y, step)
        total[...] += term(0, mid_a[source_z, y], at(y, source_z)) - term(
            1, mid_b[source_y, z], at(source_y, z)
        )

    @pl.loop(0, SIDE)
    def _(step):
        source = lax.rem(step + SIDE - 1, SIDE)
        source_z, source_y = back(z, source), back(y, source)

        @pl.loop(0, SIDE - 1)
        def _(inner):
            column, row = back(y, inner), back(z, inner)
            index_a, index_b = at(column, source_z), at(source_y, row)
            second_a(mid_a.at[source_z], source_z, column, column).wait_recv()
            second_b(mid_b.at[source_y], source_y, row, row).wait_recv()
            total[...] += term(0, in_a[index_a], index_a) - term(1, in_b[index_b], index_b)

    partial[...] = jnp.sum(total[...], axis=0, keepdims=True)

    def sum_copy(other, row):
        return remote(
            partial, gathered.at[row], sum_send_sem.at[other], sum_recv_sem.at[row], freq=other
        )

    @pl.loop(1, freqs)
    def _(k):
        sum_copy(lax.rem(mine + k, freqs), mine).start()

    gathered[mine] = partial[...]

    @pl.loop(1, SIDE)
    def _(k):
        other_z, other_y = lax.rem(z + k, SIDE), lax.rem(y + k, SIDE)
        label_copy1(other_z, z).wait_send()
        label_copy2(other_y, y).wait_send()
        first_a(other_z, z).wait_send()
        first_b(other_y, y).wait_send()

        @pl.loop(0, SIDE)
        def _(source):
            second_a(mid_a.at[source], source, other_y, y).wait_send()
            second_b(mid_b.at[source], source, other_z, z).wait_send()

    @pl.loop(1, freqs)
    def _(k):
        other = lax.rem(mine + k, freqs)
        sum_copy(other, other).wait_recv()
        sum_copy(other, mine).wait_send()

    result = gathered[0]
    for row in range(1, freqs):
        result = result + gathered[row]
    out_ref[...] = result


def count(mask, axis):
    return jnp.sum(jnp.where(mask, 1, 0), axis=axis, keepdims=True)


def iota(shape, axis):
    return lax.broadcasted_iota(jnp.int32, shape, axis)


def onehot(mask):
    return mask.astype(jnp.float32).astype(jnp.bfloat16)


def make_lists(axis_row, axis_col, slot_row, slot_col, here):
    off_row = lax.rem(axis_row - here + SIDE, SIDE)
    off_col = lax.rem(axis_col - here + SIDE, SIDE)
    half = SIDE // 2
    far_row, far_col = off_row == half, off_col == half
    index_row = count(far_col & (slot_col < slot_row), 0)
    index_col = count(far_row & (slot_row < slot_col), 1)
    number = count(far_row, 1)
    up = count((off_row >= 1) & (off_row < half), 1)
    down = count(off_row > half, 1)
    split = jnp.minimum(jnp.maximum(down + number - up, 0) // 2, number)

    def which(off, index):
        plus = ((off >= 1) & (off < half)) | ((off == half) & (index < split))
        minus = (off > half) | ((off == half) & (index >= split))
        return jnp.where(plus, 0, jnp.where(minus, 1, 2))

    list_row, list_col = which(off_row, index_row), which(off_col, index_col)
    dist_row = jnp.minimum(off_row, SIDE - off_row)
    dist_col = jnp.minimum(off_col, SIDE - off_col)
    key_row = (half - dist_row) * (SIDE * SLOTS) + slot_row
    key_col = (half - dist_col) * (SIDE * SLOTS) + slot_col
    place = count((list_col == list_row) & (key_col < key_row), 0)

    over = jnp.zeros((1, 1), jnp.int32)
    for one in range(2):
        for step in range(STEPS):
            length = count((list_row == one) & (dist_row > step), 1)
            over = jnp.maximum(over, jnp.where(length > CAPS[step], 1, 0))

    row = lax.rem(iota((SIDE, 1), 0) - here + SIDE, SIDE)
    row_list = jnp.where(row < half, 0, 1)
    row_dist = jnp.minimum(row, SIDE - row)
    start = count((list_row == row_list) & (dist_row > row_dist), 1)
    return list_row, place, start, split, over


def compact_kernel(
    freqs, columns_ref, target_ref, receiver_ref, panels_hbm, fields_hbm, blocks_hbm,
    out_ref, flag_ref,
    stored, panels, fields, blocks, lists, ring1, ring2, ring3, ring4, mid_a, mid_b, in_a, in_b,
    labels_own, labels_mid, labels_in, dense, left, product, total, partial, gathered,
    load_sem, label_send1, label_recv1, label_send2, label_recv2, hop_send, hop_recv,
    send2_a, recv2_a, send2_b, recv2_b, sum_send_sem, sum_recv_sem,
):
    me = lax.axis_index("brick")
    mine = lax.axis_index("freq")
    z, y = me // SIDE, lax.rem(me, SIDE)
    here = (z, y)
    rings = (ring1, ring2, ring3, ring4)
    mids = (mid_a, mid_b)
    held = panels.shape[1]
    span = fields.shape[1]
    cells = span // 3
    tx = fields.shape[0] // 2
    group = SIDE * SLOTS

    def remote(src, dst, send, recv, **where):
        return pltpu.make_async_remote_copy(
            src_ref=src, dst_ref=dst, send_sem=send, recv_sem=recv,
            device_id=where, device_id_type=MESH,
        )

    def at(row, column):
        return row * SIDE + column

    def along(path, other):
        return at(other, y) if path == 0 else at(z, other)

    def around(start, step):
        return lax.rem(start + zigzag(step), SIDE)

    def back(start, step):
        return lax.rem(start - zigzag(step) + SIDE, SIDE)

    loads = [
        pltpu.make_async_copy(panels_hbm, stored, load_sem.at[0]),
        pltpu.make_async_copy(blocks_hbm, blocks, load_sem.at[1]),
        pltpu.make_async_copy(fields_hbm, fields, load_sem.at[2]),
    ]
    for load in loads:
        load.start()

    barrier = pltpu.get_barrier_semaphore()

    @pl.loop(1, SIDE)
    def _(k):
        for path in range(2):
            other = lax.rem(here[path] + k, SIDE)
            pl.semaphore_signal(
                barrier, inc=1, device_id={"brick": along(path, other)}, device_id_type=MESH
            )

    @pl.loop(1, freqs)
    def _(k):
        pl.semaphore_signal(
            barrier, inc=1, device_id={"freq": lax.rem(mine + k, freqs)}, device_id_type=MESH
        )

    target = target_ref[...]
    down, across = iota((held, held), 0), iota((held, held), 1)
    target_col = jnp.sum(jnp.where(down == across, target, 0), axis=1, keepdims=True)
    same = target_col == target
    rank, rank_col = count(same & (down < across), 0), count(same & (across < down), 1)
    axis_row = (target // SIDE, lax.rem(target, SIDE))
    axis_col = (target_col // SIDE, lax.rem(target_col, SIDE))
    slot_row = tuple(axis_row[1 - path] * SLOTS + rank for path in range(2))
    slot_col = tuple(axis_col[1 - path] * SLOTS + rank_col for path in range(2))

    loads[0].wait()
    panels[...] = jnp.swapaxes(stored[...], 0, 1)
    value = receiver_ref[...] + 1
    over = jnp.zeros((1, 1), jnp.int32)
    lanes = iota((SIDE, 128), 1)
    rows = []
    for path in range(2):
        list_row, place, start, split, too_long = make_lists(
            axis_row[path], axis_col[path], slot_row[path], slot_col[path], here[path]
        )
        over = jnp.maximum(over, too_long)
        for one in range(2):
            select = onehot((iota((CAPS[0], held), 0) == place) & (list_row == one))
            found = jnp.dot(select, panels[path], preferred_element_type=jnp.float32)
            found = found.reshape(CAPS[0] // SLOTS, SLOTS, span)
            lists[2 * path + one] = found.astype(jnp.bfloat16)
        names = iota((SIDE, held), 0) == axis_row[path]
        by_lane = onehot(slot_col[path] == iota((held, 128), 1))
        high = jnp.where(names, value // 16, 0).astype(jnp.float32).astype(jnp.bfloat16)
        low = jnp.where(names, lax.rem(value, 16), 0).astype(jnp.float32).astype(jnp.bfloat16)
        high = jnp.dot(high, by_lane, preferred_element_type=jnp.float32)
        low = jnp.dot(low, by_lane, preferred_element_type=jnp.float32)
        named = (high * 16.0 + low).astype(jnp.int32)
        named = jnp.where(lanes == START_LANE, start, named)
        rows.append(jnp.where(lanes == SPLIT_LANE, split, named))
    labels_own[0] = jnp.where(lanes == FLAG_LANE, over, rows[0])
    labels_own[1] = rows[1]

    def label_copy1(path, other, row):
        return remote(
            labels_own.at[path, pl.ds(other, 1)], labels_mid.at[path, pl.ds(row, 1)],
            label_send1.at[path, other], label_recv1.at[path, row],
            brick=along(path, other),
        )

    def label_copy2(other, row):
        return remote(
            labels_mid.at[0], labels_in.at[row],
            label_send2.at[other], label_recv2.at[row], brick=at(z, other),
        )

    def hop(path, one, step, chunk):
        part = 2 * path + one
        piece = pl.ds(EDGES[chunk] // SLOTS, (EDGES[chunk + 1] - EDGES[chunk]) // SLOTS)
        source = lists if step == 0 else rings[step - 1]
        index = (part * STEPS + step) * STEPS + chunk
        other = lax.rem(here[path] + (1 if one == 0 else SIDE - 1), SIDE)
        return remote(
            source.at[part, piece], rings[step].at[part, piece],
            hop_send.at[index], hop_recv.at[index], brick=along(path, other),
        )

    ways = [(path, one) for path in range(2) for one in range(2)]

    def second_a(source, other, column):
        index = at(column, source)
        return remote(
            mid_a.at[source, other], in_a.at[index],
            send2_a.at[at(source, other)], recv2_a.at[index], brick=at(z, other),
        )

    def second_b(source, other, row):
        index = at(source, row)
        return remote(
            mid_b.at[source, other], in_b.at[index],
            send2_b.at[at(source, other)], recv2_b.at[index], brick=at(other, y),
        )

    def pass_on(path, source):
        @pl.loop(0, SIDE - 1)
        def _(inner):
            if path == 0:
                second_a(source, around(y, inner), y).start()
            else:
                second_b(source, around(z, inner), z).start()

    def spread(path, step, one):
        source = lax.rem(here[path] + (SIDE - step - 1 if one == 0 else step + 1), SIDE)
        row = labels_mid[path, pl.ds(source, 1)]
        lane, slot = iota((group, 128), 1), iota((group, 128), 0)
        filled = row > 0
        full = count((lane == slot) & filled, 1) > 0
        index = count((lane < slot) & filled, 1)
        single = iota((1, 128), 1)
        if step < STEPS - 1:
            index = index + jnp.sum(jnp.where(single == START_LANE, row, 0), axis=1, keepdims=True)
        else:
            split = jnp.sum(jnp.where(single == SPLIT_LANE, row, 0), axis=1, keepdims=True)
            if one == 0:
                full = full & (index < split)
            else:
                full = full & (index >= split)
                index = index - split
        select = onehot((iota((group, CAPS[step]), 1) == index) & full)
        rows = rings[step][2 * path + one].astype(jnp.float32).reshape(CAPS[step], span)
        return source, jnp.dot(
            select, rows.astype(jnp.bfloat16), preferred_element_type=jnp.float32
        )

    def put(path, source, found):
        mids[path][source] = found.reshape(SIDE, SLOTS, span).astype(jnp.bfloat16)

    def deliver(step):
        if step < STEPS - 1:
            for one in range(2):
                for path in range(2):
                    source, found = spread(path, step, one)
                    put(path, source, found)
                    pass_on(path, source)
        else:
            for path in range(2):
                source, found = spread(path, step, 0)
                put(path, source, found + spread(path, step, 1)[1])
                pass_on(path, source)

    def receive(step):
        for chunk in range(STEPS - step):
            for path, one in ways:
                hop(path, one, step, chunk).wait_recv()
                if chunk < STEPS - step - 1:
                    hop(path, one, step + 1, chunk).start()

    pl.semaphore_wait(barrier, 2 * (SIDE - 1) + freqs - 1)

    @pl.loop(1, SIDE)
    def _(k):
        for path in range(2):
            label_copy1(path, lax.rem(here[path] + k, SIDE), here[path]).start()

    for chunk in range(STEPS):
        for path, one in ways:
            hop(path, one, 0, chunk).start()

    for path in range(2):
        select = onehot((iota((group, held), 0) == slot_row[path]) & (axis_row[path] == here[path]))
        put(path, here[path], jnp.dot(select, panels[path], preferred_element_type=jnp.float32))
        labels_mid[path, pl.ds(here[path], 1)] = labels_own[path, pl.ds(here[path], 1)]

    @pl.loop(1, SIDE)
    def _(k):
        for path in range(2):
            other = lax.rem(here[path] + k, SIDE)
            label_copy1(path, other, other).wait_recv()

    @pl.loop(1, SIDE)
    def _(k):
        label_copy2(lax.rem(y + k, SIDE), y).start()

    labels_in[y] = labels_mid[0]

    receive(0)
    for path in range(2):
        pass_on(path, here[path])
    deliver(0)

    loads[1].wait()
    for k in range(columns_ref.shape[2]):
        for r in range(SIDE):
            tile = jnp.zeros((blocks.shape[2], blocks.shape[3]), jnp.bfloat16)
            for j in range(columns_ref.shape[0]):
                tile = jnp.where(columns_ref[j, 0, k] == r, blocks[k, j], tile)
            dense[0, pl.ds(k * 64, 64), pl.ds(r * 64, 64)] = tile[:, :64]
            dense[1, pl.ds(k * 64, 64), pl.ds(r * 64, 64)] = tile[:, 64:]

    receive(1)
    deliver(1)

    @pl.loop(1, SIDE)
    def _(k):
        other = lax.rem(y + k, SIDE)
        label_copy2(other, other).wait_recv()

    slots = SIDE * group
    named = labels_in[...].reshape(SIDE * SIDE, 128)
    flags = jnp.where(iota((SIDE * SIDE, 128), 1) == FLAG_LANE, named, 0)
    flag = jnp.max(jnp.max(flags, axis=1, keepdims=True), axis=0, keepdims=True)
    flag_ref[...] = jnp.broadcast_to(flag, flag_ref.shape)
    pick = iota((SIDE * SIDE, SLOTS, 128), 1) + y * SLOTS == iota((SIDE * SIDE, SLOTS, 128), 2)
    label = jnp.sum(jnp.where(pick, named[:, None, :], 0), axis=2, keepdims=True)
    label = label.reshape(slots, 1) - 1
    chosen = onehot(iota((slots, dense.shape[2]), 1) == label)
    dims = (((1,), (1,)), ((), ()))
    real = lax.dot_general(chosen, dense[0], dims, preferred_element_type=jnp.float32)
    imag = lax.dot_general(chosen, dense[1], dims, preferred_element_type=jnp.float32)
    left[0, :, pl.ds(0, tx)] = real.astype(jnp.bfloat16)
    left[0, :, pl.ds(tx, tx)] = (-imag).astype(jnp.bfloat16)
    left[1, :, pl.ds(0, tx)] = imag.astype(jnp.bfloat16)
    left[1, :, pl.ds(tx, tx)] = real.astype(jnp.bfloat16)

    receive(2)
    deliver(2)
    receive(3)
    deliver(3)

    loads[2].wait()

    @pl.loop(0, SIDE)
    def _(piece):
        part, tile = piece // 4, lax.rem(piece, 4)
        rows = pl.ds(pl.multiple_of(tile * 128, 128), 128)
        product[part, rows] = jnp.dot(
            left[part, rows], fields[...], preferred_element_type=jnp.float32
        )

    def term(part, block, index):
        rows = pl.ds(pl.multiple_of(index * SLOTS, SLOTS), SLOTS)
        both = product[part, rows] * block.astype(jnp.float32)
        return both[:, :cells] + both[:, cells : 2 * cells] + both[:, 2 * cells :]

    total[...] = jnp.zeros_like(total)

    @pl.loop(0, SIDE)
    def _(source):
        total[...] += term(0, mid_a[source, y], at(y, source)) - term(
            1, mid_b[source, z], at(source, z)
        )

    @pl.loop(0, SIDE)
    def _(step):
        source_z, source_y = back(z, SIDE - 1 - step), back(y, SIDE - 1 - step)

        @pl.loop(0, SIDE - 1)
        def _(inner):
            column, row = back(y, inner), back(z, inner)
            index_a, index_b = at(column, source_z), at(source_y, row)
            second_a(source_z, column, column).wait_recv()
            second_b(source_y, row, row).wait_recv()
            total[...] += term(0, in_a[index_a], index_a) - term(1, in_b[index_b], index_b)

    partial[...] = jnp.sum(total[...], axis=0, keepdims=True)

    def sum_copy(other, row):
        return remote(
            partial, gathered.at[row], sum_send_sem.at[other], sum_recv_sem.at[row], freq=other
        )

    @pl.loop(1, freqs)
    def _(k):
        sum_copy(lax.rem(mine + k, freqs), mine).start()

    gathered[mine] = partial[...]

    for step in range(STEPS):
        for chunk in range(STEPS - step):
            for path, one in ways:
                hop(path, one, step, chunk).wait_send()

    @pl.loop(1, SIDE)
    def _(k):
        other_z, other_y = lax.rem(z + k, SIDE), lax.rem(y + k, SIDE)
        label_copy1(0, other_z, z).wait_send()
        label_copy1(1, other_y, y).wait_send()
        label_copy2(other_y, y).wait_send()

        @pl.loop(0, SIDE)
        def _(source):
            second_a(source, other_y, y).wait_send()
            second_b(source, other_z, z).wait_send()

    @pl.loop(1, freqs)
    def _(k):
        other = lax.rem(mine + k, freqs)
        sum_copy(other, other).wait_recv()
        sum_copy(other, mine).wait_send()

    result = gathered[0]
    for row in range(1, freqs):
        result = result + gathered[row]
    out_ref[...] = result


def on_device(
    forward_fields, adjoint_panels, residual_blocks, residual_columns, panel_brick, panel_receiver
):
    bricks, freqs = lax.axis_size("brick"), lax.axis_size("freq")
    held, span = adjoint_panels.shape[1], adjoint_panels.shape[3]
    cells = span // 3
    tx = forward_fields.shape[3]
    fields = forward_fields[0, 0].reshape(2 * tx, span)
    blocks = residual_blocks[0, 0]
    slots = bricks * SLOTS
    half = (SIDE, SIDE, SLOTS, span)
    any_space = pl.BlockSpec(memory_space=pl.ANY)
    vmem = pl.BlockSpec(memory_space=pltpu.VMEM)
    in_specs = [
        pl.BlockSpec(memory_space=pltpu.SMEM), vmem, vmem, any_space, any_space, any_space,
    ]
    loaded = [
        pltpu.VMEM((held, 2, span), jnp.bfloat16),
        pltpu.VMEM((2, held, span), jnp.bfloat16),
        pltpu.VMEM(fields.shape, jnp.bfloat16),
        pltpu.VMEM(blocks.shape, jnp.bfloat16),
    ]
    halves = [pltpu.VMEM(half, jnp.bfloat16)] * 2
    arrived = [pltpu.VMEM((bricks, SLOTS, span), jnp.bfloat16)] * 2
    work = [
        pltpu.VMEM((2, tx, 512), jnp.bfloat16),
        pltpu.VMEM((2, slots, 2 * tx), jnp.bfloat16),
        pltpu.VMEM((2, slots, span), jnp.float32),
        pltpu.VMEM((SLOTS, cells), jnp.float32),
        pltpu.VMEM((1, cells), jnp.float32),
        pltpu.VMEM((freqs, 1, cells), jnp.float32),
    ]

    def dma(*shape):
        return pltpu.SemaphoreType.DMA(shape)

    args = (
        residual_columns.transpose(2, 0, 1),
        panel_brick.reshape(1, held),
        panel_receiver.reshape(1, held),
        adjoint_panels[0],
        fields,
        blocks,
    )
    gradient = jax.ShapeDtypeStruct((1, cells), jnp.float32)
    summed, flag = pl.pallas_call(
        functools.partial(compact_kernel, freqs),
        out_shape=[gradient, jax.ShapeDtypeStruct((1, 128), jnp.int32)],
        in_specs=in_specs,
        out_specs=[vmem, vmem],
        scratch_shapes=[
            *loaded,
            pltpu.VMEM((4, CAPS[0] // SLOTS, SLOTS, span), jnp.bfloat16),
            *[pltpu.VMEM((4, cap // SLOTS, SLOTS, span), jnp.bfloat16) for cap in CAPS],
            *halves,
            *arrived,
            pltpu.VMEM((2, SIDE, 128), jnp.int32),
            pltpu.VMEM((2, SIDE, 128), jnp.int32),
            pltpu.VMEM((SIDE, SIDE, 128), jnp.int32),
            *work,
            dma(3),
            *[dma(2, SIDE)] * 2,
            *[dma(SIDE)] * 2,
            *[dma(4 * STEPS * STEPS)] * 2,
            *[dma(bricks)] * 4,
            *[dma(freqs)] * 2,
        ],
        compiler_params=pltpu.CompilerParams(collective_id=0, has_side_effects=True),
        name="compact_exchange",
    )(*args)

    def padded():
        return pl.pallas_call(
            functools.partial(padded_kernel, freqs),
            out_shape=gradient,
            in_specs=in_specs,
            out_specs=vmem,
            scratch_shapes=[
                *loaded,
                *halves,
                *halves,
                *arrived,
                pltpu.VMEM((SIDE, 128), jnp.int32),
                pltpu.VMEM((SIDE, 128), jnp.int32),
                pltpu.VMEM((SIDE, SIDE, 128), jnp.int32),
                *work,
                dma(3),
                *[dma(SIDE)] * 8,
                *[dma(bricks)] * 4,
                *[dma(freqs)] * 2,
            ],
            compiler_params=pltpu.CompilerParams(collective_id=1, has_side_effects=True),
            name="padded_exchange",
        )(*args)

    summed = lax.cond(flag[0, 0] > 0, padded, lambda: summed)
    share = cells // freqs
    return lax.dynamic_slice_in_dim(summed[0], lax.axis_index("freq") * share, share, 0)


def solution(mesh):
    placed = (
        P("freq", "brick", None, None, None),
        P("freq", "brick", None, None),
        P("freq", "brick", None, None, None, None),
        P("brick", None, None),
        P("brick", None),
        P("brick"),
    )
    return jax.shard_map(
        on_device, mesh=mesh, in_specs=placed, out_specs=P(("brick", "freq")), check_vma=False
    )
```
